32 devices in a mesh: rows: 4 (over x, core), labels: 8 (over z, y).
Axes of the slice: x: 2, y: 2, z: 4, core: 2. Of those that a mesh axis runs over, the one named last changes fastest.
Arguments:
- pool_features: bfloat16 [512, 768], P('rows'), may hold values from -6 to 6
- pool_labels: int32 [512, 16], P('rows'), may hold values from 0 to 12287
- pool_counts: int32 [512], P('rows'), may hold values from 1 to 16
- batch_rows: int32 [2, 128], P(None, 'rows'), may hold values from 0 to 127
- weights: float32 [12288, 768], P(('rows', 'labels')), may hold values from -0.21875 to 0.21875
- momentum: float32 [12288, 768], P(('rows', 'labels')), may hold values from -24 to 24
Outputs:
- new_weights: float32 [12288, 768], P(('rows', 'labels'))
- new_momentum: float32 [12288, 768], P(('rows', 'labels'))
- feature_grads: float32 [2, 128, 768], P(None, 'rows')
The draws below stay inside these ranges and needn't reach their ends.
Inputs may be any that keep to these rules, and one draw needn't show every extreme that they name: `pool_labels`: slots of a list at or past its count are padding and are ignored; a label may appear twice in a list. `batch_rows`: an entry names one of the 128 examples stored with the index of rows that owns that batch row.
All inputs are finite; a program needn't handle non-finite values.
Results may differ from the reference program's by a relative error of at most 0.00045.
The reference program's roundings to bfloat16 on the way count: a program that leaves them out, or rounds other values in their place, can miss the bound.
Values may be sent and summed in bfloat16 or wider, within the bound.
No kernel may reach another device: no remote copies, remote signals or barrier semaphores. Data moves between devices by JAX's collectives and lax.ppermute only.
A program may use at most 64 MiB of HBM per device.

```python
import jax
import jax.numpy as jnp
from jax import lax

D = 768
LAB_DEV = 384
P_SIZE = 16
ROW_GRP = 32
POOL_ROW = 128
B = 128
LABELS = 12288
EXAMPLES = 512


def touch_ends(array, key, low, largest):
    index_at = [jax.random.randint(jax.random.fold_in(key, axis), (), 0, length) for axis, length in enumerate(array.shape)]
    widest = array.shape.index(max(array.shape))
    next_to = index_at[:widest] + [(index_at[widest] + 1) % array.shape[widest]] + index_at[widest + 1:]
    return array.at[tuple(index_at)].set(low).at[tuple(next_to)].set(largest)


def shard_levels(rng, shape, split, smallest, top_value):
    def one(dim, blocks):
        heights = jax.random.uniform(jax.random.fold_in(jax.random.fold_in(rng, 6), dim), (blocks,), jnp.float32, smallest / len(split), top_value / len(split))
        return jnp.repeat(jnp.exp(heights), shape[dim] // blocks).reshape((-1,) + (1,) * (len(shape) - dim - 1))

    level = one(*split[0])
    for cut in split[1:]:
        level = level * one(*cut)
    return level


def scatter_about(rng, extent, spread, most, shards=(), kind=jnp.bfloat16):
    values = spread * jax.random.normal(rng, extent, jnp.float32)
    if shards:
        values = values * shard_levels(rng, extent, shards, -0.22, 0.18)
    return jnp.clip(values, -most, most).astype(kind)


def setup_inputs(seed: int = 0) -> dict:
    key_of = jax.random.split(jax.random.key(seed), 7)
    pool_features = scatter_about(key_of[0], (EXAMPLES, D), 1.0, 6.0, ((0, 4),))
    pool_labels = touch_ends(jax.random.randint(key_of[1], (EXAMPLES, P_SIZE), 0, LABELS), jax.random.fold_in(key_of[1], 1), 0, LABELS - 1).astype(jnp.int32)
    pool_counts = touch_ends(jax.random.randint(key_of[2], (EXAMPLES,), 1, P_SIZE + 1), jax.random.fold_in(key_of[2], 1), 1, P_SIZE).astype(jnp.int32)
    batch_rows = touch_ends(jax.random.randint(key_of[3], (2, B), 0, POOL_ROW), jax.random.fold_in(key_of[3], 1), 0, POOL_ROW - 1).astype(jnp.int32)
    weights = scatter_about(key_of[4], (LABELS, D), D ** -0.5, 0.21875, ((0, 32),), jnp.float32)
    momentum = scatter_about(key_of[5], (LABELS, D), 4.0, 24.0, ((0, 32),), jnp.float32)
    return {"pool_features": pool_features, "pool_labels": pool_labels, "pool_counts": pool_counts, "batch_rows": batch_rows, "weights": weights, "momentum": momentum}


learn_rate = 0.001
decay_rate = 0.9


def batch_step(features, label_ids, counts, weights, momentum):
    blocks = weights.reshape(-1, LAB_DEV, D)
    moments = momentum.reshape(-1, LAB_DEV, D)
    in_list = jnp.arange(label_ids.shape[1], dtype=jnp.int32)[None, :] < counts[:, None]

    def block_step(summed, pieces):
        weight_block, moment_block, block_index = pieces
        low_weights = weight_block.astype(jnp.bfloat16)
        logits = lax.dot_general(features, low_weights, (((1,), (1,)), ((), ())), preferred_element_type=jnp.float32)
        labels = block_index * LAB_DEV + jnp.arange(LAB_DEV, dtype=jnp.int32)
        matched = (label_ids[:, :, None] == labels[None, None, :]) & in_list[:, :, None]
        targets = jnp.any(matched, axis=1).astype(jnp.float32)
        errors = (jax.nn.sigmoid(logits) - targets).astype(jnp.bfloat16)
        grads = lax.dot_general(errors, features, (((0,), (0,)), ((), ())), preferred_element_type=jnp.float32)
        summed = summed + jnp.dot(errors, low_weights, preferred_element_type=jnp.float32)
        moment_block = decay_rate * moment_block + grads
        weight_block = weight_block - learn_rate * moment_block
        return summed, (weight_block, moment_block)

    start = jnp.zeros((features.shape[0], D), jnp.float32)
    indices = jnp.arange(blocks.shape[0], dtype=jnp.int32)
    summed, (blocks, moments) = lax.scan(block_step, start, (blocks, moments, indices))
    return summed, blocks.reshape(-1, D), moments.reshape(-1, D)


def reference(pool_features, pool_labels, pool_counts, batch_rows, weights, momentum):
    owners = (jnp.arange(B, dtype=jnp.int32) // ROW_GRP) * POOL_ROW
    results = []
    for batch in range(2):
        chosen = owners + batch_rows[batch]
        summed, weights, momentum = batch_step(pool_features[chosen], pool_labels[chosen], pool_counts[chosen], weights, momentum)
        results.append(summed)
    return weights, momentum, jnp.stack(results)
```

```python
import functools

import jax
import jax.numpy as jnp
from jax import lax
from jax.experimental import pallas as pl
from jax.experimental.pallas import tpu as pltpu
from jax.sharding import PartitionSpec as P

learn_rate = 0.001
decay_rate = 0.9
LANES = 128
DIGITS = 3
NO_LABEL = 255
VMEM_LIMIT = 16 << 20


def select_kernel(rows_ref, features_ref, labels_ref, counts_ref, out_ref):
    slots, stored = labels_ref.shape
    batches, group = rows_ref.shape
    width = features_ref.shape[1]
    ids = labels_ref[...]
    used = lax.broadcasted_iota(jnp.int32, (slots, stored), 0) < counts_ref[...]
    digits = [ids & 255, (ids >> 8) & 255, jnp.where(used, ids >> 16, NO_LABEL)]
    spare = LANES - DIGITS * slots
    table = jnp.concatenate(
        [d.astype(jnp.float32) for d in digits] + [jnp.zeros((spare, stored), jnp.float32)], axis=0
    ).astype(jnp.bfloat16)
    features = features_ref[...]
    for t in range(batches):
        chosen = lax.broadcasted_iota(jnp.int32, (stored, group), 0) == rows_ref[t : t + 1, :]
        one_hot = jnp.transpose(chosen.astype(jnp.float32)).astype(jnp.bfloat16)
        out_ref[t * group : (t + 1) * group, :width] = jnp.dot(
            one_hot, features, preferred_element_type=jnp.float32
        ).astype(jnp.bfloat16)
        out_ref[t * group : (t + 1) * group, width:] = lax.dot_general(
            one_hot, table, (((1,), (1,)), ((), ())), preferred_element_type=jnp.float32
        ).astype(jnp.bfloat16)


def batch_errors(features, codes, low_weights, base, slots):
    logits = lax.dot_general(
        features, low_weights, (((1,), (1,)), ((), ())), preferred_element_type=jnp.float32
    )
    codes = codes.astype(jnp.float32)
    ids = codes[:, :slots] + 256.0 * codes[:, slots : 2 * slots] + 65536.0 * codes[:, 2 * slots : 3 * slots]
    local = (ids - base).astype(jnp.int32)
    lane = lax.broadcasted_iota(jnp.int32, logits.shape, 1)
    hit = lane == local[:, 0:1]
    for k in range(1, slots):
        hit = hit | (lane == local[:, k : k + 1])
    targets = jnp.where(hit, 1.0, 0.0)
    return (jax.nn.sigmoid(logits) - targets).astype(jnp.bfloat16)


def grads_of(errors, features):
    return lax.dot_general(
        errors, features, (((0,), (0,)), ((), ())), preferred_element_type=jnp.float32
    )


def parts_kernel(base_ref, *refs, pieces, group, slots):
    piece_refs = refs[:pieces]
    weights_ref, momentum_ref = refs[pieces : pieces + 2]
    parts_ref, errors_ref, last_ref, weights_out, momentum_out = refs[pieces + 2 :]
    width = weights_ref.shape[1]
    base = base_ref[0].astype(jnp.float32)

    def batch(t):
        rows = jnp.concatenate([r[t * group : (t + 1) * group, :] for r in piece_refs], axis=0)
        return rows[:, :width], rows[:, width:]

    def put(t, low_weights, errors):
        summed = jnp.dot(errors, low_weights, preferred_element_type=jnp.float32)
        for p in range(pieces):
            start = (2 * p + t) * group
            parts_ref[start : start + group, :] = summed[p * group : (p + 1) * group, :]

    features, codes = batch(0)
    weights = weights_ref[...]
    low_weights = weights.astype(jnp.bfloat16)
    errors = batch_errors(features, codes, low_weights, base, slots)
    put(0, low_weights, errors)
    momentum = decay_rate * momentum_ref[...] + grads_of(errors, features)
    weights = weights - learn_rate * momentum
    momentum_out[...] = momentum
    weights_out[...] = weights
    features, codes = batch(1)
    low_weights = weights.astype(jnp.bfloat16)
    errors = batch_errors(features, codes, low_weights, base, slots)
    put(1, low_weights, errors)
    errors_ref[...] = errors
    last_ref[...] = features


def update_kernel(errors_ref, features_ref, weights_ref, momentum_ref, weights_out, momentum_out):
    momentum = decay_rate * momentum_ref[...] + grads_of(errors_ref[...], features_ref[...])
    momentum_out[...] = momentum
    weights_out[...] = weights_ref[...] - learn_rate * momentum


def swap(x, axis, mask):
    size = lax.axis_size(axis)
    return lax.ppermute(x, axis, [(i, i ^ mask) for i in range(size)])


def masks_of(axis):
    size = lax.axis_size(axis)
    return [1 << b for b in range(size.bit_length() - 1)]


def per_device(pool_features, pool_labels, pool_counts, batch_rows, weights, momentum):
    labels, width = weights.shape
    stored, slots = pool_labels.shape
    batches, group = batch_rows.shape
    pieces = lax.axis_size("rows")
    batch_size = pieces * group
    device_index = lax.axis_index("rows") * lax.axis_size("labels") + lax.axis_index("labels")
    base = (device_index * labels).astype(jnp.int32).reshape(1)
    vmem = pl.BlockSpec(memory_space=pltpu.VMEM)
    params = pltpu.CompilerParams(vmem_limit_bytes=VMEM_LIMIT)

    own = pl.pallas_call(
        select_kernel,
        out_shape=jax.ShapeDtypeStruct((batches * group, width + LANES), jnp.bfloat16),
        in_specs=[vmem] * 4,
        out_specs=vmem,
        compiler_params=params,
        name="select_rows",
    )(batch_rows, pool_features, pool_labels.T, pool_counts.reshape(1, stored))

    gathered = [own]
    for mask in reversed(masks_of("rows")):
        gathered = gathered + [swap(g, "rows", mask) for g in gathered]

    parts, errors, last, weights, momentum = pl.pallas_call(
        functools.partial(parts_kernel, pieces=pieces, group=group, slots=slots),
        out_shape=(
            jax.ShapeDtypeStruct((batches * batch_size, width), jnp.float32),
            jax.ShapeDtypeStruct((batch_size, labels), jnp.bfloat16),
            jax.ShapeDtypeStruct((batch_size, width), jnp.bfloat16),
            jax.ShapeDtypeStruct(weights.shape, jnp.float32),
            jax.ShapeDtypeStruct(momentum.shape, jnp.float32),
        ),
        in_specs=[pl.BlockSpec(memory_space=pltpu.SMEM)] + [vmem] * (pieces + 2),
        out_specs=(vmem,) * 5,
        compiler_params=params,
        name="parts",
    )(base, *gathered, weights, momentum)

    weights, momentum = pl.pallas_call(
        update_kernel,
        out_shape=(
            jax.ShapeDtypeStruct(weights.shape, jnp.float32),
            jax.ShapeDtypeStruct(momentum.shape, jnp.float32),
        ),
        in_specs=[vmem] * 4,
        out_specs=(vmem,) * 2,
        compiler_params=params,
        cost_estimate=pl.CostEstimate(
            flops=2 * batch_size * labels * width, transcendentals=0, bytes_accessed=16 * labels * width
        ),
        name="last_update",
    )(errors, last, weights, momentum)

    for mask in masks_of("rows"):
        half = parts.shape[0] // 2
        parts = parts[:half] + swap(parts[half:], "rows", mask)
    for mask in masks_of("labels"):
        parts = parts + swap(parts, "labels", mask)
    return weights, momentum, parts.reshape(batches, group, width)


def solution(mesh):
    in_specs = (
        P("rows", None),
        P("rows", None),
        P("rows"),
        P(None, "rows"),
        P(("rows", "labels"), None),
        P(("rows", "labels"), None),
    )
    out_specs = (P(("rows", "labels"), None), P(("rows", "labels"), None), P(None, "rows", None))
    return jax.shard_map(
        per_device, mesh=mesh, in_specs=in_specs, out_specs=out_specs, check_vma=False
    )
```

```python
import functools
import math

import jax
import jax.numpy as jnp
from jax import lax
from jax.experimental import pallas as pl
from jax.experimental.pallas import tpu as pltpu
from jax.sharding import PartitionSpec as P

learn_rate = 0.001
decay_rate = 0.9
LANES = 128
DIGITS = 3
NO_LABEL = 255
VMEM_LIMIT = 16 << 20
TILE_ROWS = 16
CODE_TOP = 32000.0
SMALLEST = 1e-30


def fetch(sources, targets, sems):
    copies = [pltpu.make_async_copy(s, t, sems.at[i]) for i, (s, t) in enumerate(zip(sources, targets))]
    for copy in copies:
        copy.start()
    return copies


def select_kernel(rows_hbm, features_hbm, labels_hbm, counts_hbm, out_ref, rows_ref, features_ref, labels_ref, counts_ref, sems):
    copies = fetch(
        (rows_hbm, features_hbm, labels_hbm, counts_hbm), (rows_ref, features_ref, labels_ref, counts_ref), sems
    )
    for copy in copies:
        copy.wait()
    slots, stored = labels_ref.shape
    batches, group = rows_ref.shape
    width = features_ref.shape[1]
    ids = labels_ref[...]
    used = lax.broadcasted_iota(jnp.int32, (slots, stored), 0) < counts_ref[...]
    digits = [ids & 255, (ids >> 8) & 255, jnp.where(used, ids >> 16, NO_LABEL)]
    spare = LANES - DIGITS * slots
    table = jnp.concatenate(
        [d.astype(jnp.float32) for d in digits] + [jnp.zeros((spare, stored), jnp.float32)], axis=0
    ).astype(jnp.bfloat16)
    features = features_ref[...]
    for t in range(batches):
        chosen = lax.broadcasted_iota(jnp.int32, (stored, group), 0) == rows_ref[t : t + 1, :]
        one_hot = jnp.transpose(chosen.astype(jnp.float32)).astype(jnp.bfloat16)
        out_ref[t * group : (t + 1) * group, :width] = jnp.dot(
            one_hot, features, preferred_element_type=jnp.float32
        ).astype(jnp.bfloat16)
        out_ref[t * group : (t + 1) * group, width:] = lax.dot_general(
            one_hot, table, (((1,), (1,)), ((), ())), preferred_element_type=jnp.float32
        ).astype(jnp.bfloat16)


def batch_errors(features, codes, low_weights, base, slots):
    logits = lax.dot_general(
        features, low_weights, (((1,), (1,)), ((), ())), preferred_element_type=jnp.float32
    )
    codes = codes.astype(jnp.float32)
    ids = codes[:, :slots] + 256.0 * codes[:, slots : 2 * slots] + 65536.0 * codes[:, 2 * slots : 3 * slots]
    local = (ids - base).astype(jnp.int32)
    lane = lax.broadcasted_iota(jnp.int32, logits.shape, 1)
    hit = lane == local[:, 0:1]
    for k in range(1, slots):
        hit = hit | (lane == local[:, k : k + 1])
    targets = jnp.where(hit, 1.0, 0.0)
    return (jax.nn.sigmoid(logits) - targets).astype(jnp.bfloat16)


def grads_of(errors, features):
    return lax.dot_general(
        errors, features, (((0,), (0,)), ((), ())), preferred_element_type=jnp.float32
    )


def prepare_kernel(weights_hbm, momentum_hbm, after_ref, weights_ref, momentum_ref, low_ref, sems):
    copies = fetch((weights_hbm, momentum_hbm), (weights_ref, momentum_ref), sems)
    copies[0].wait()
    low_ref[...] = weights_ref[...].astype(jnp.bfloat16)
    copies[1].wait()


def parts_kernel(base_ref, *refs, pieces, group, slots):
    piece_refs = refs[:pieces]
    weights_ref, momentum_ref, low_ref = refs[pieces : pieces + 3]
    kept_ref, sent_ref, errors_ref, last_ref, weights_out, momentum_out = refs[pieces + 3 :]
    width = weights_ref.shape[1]
    base = base_ref[0].astype(jnp.float32)

    def batch(t):
        rows = jnp.concatenate([r[t * group : (t + 1) * group, :] for r in piece_refs], axis=0)
        return rows[:, :width], rows[:, width:]

    def put(t, low_weights, errors):
        summed = jnp.dot(errors, low_weights, preferred_element_type=jnp.float32)
        for p in range(pieces):
            half_ref = kept_ref if 2 * p < pieces else sent_ref
            start = (2 * (p % (pieces // 2)) + t) * group
            half_ref[start : start + group, :] = summed[p * group : (p + 1) * group, :]

    features, codes = batch(0)
    low_weights = low_ref[...]
    errors = batch_errors(features, codes, low_weights, base, slots)
    put(0, low_weights, errors)
    momentum = decay_rate * momentum_ref[...] + grads_of(errors, features)
    weights = weights_ref[...] - learn_rate * momentum
    momentum_out[...] = momentum
    weights_out[...] = weights
    features, codes = batch(1)
    low_weights = weights.astype(jnp.bfloat16)
    errors = batch_errors(features, codes, low_weights, base, slots)
    put(1, low_weights, errors)
    errors_ref[...] = errors
    last_ref[...] = features


def update_kernel(errors_ref, features_ref, weights_ref, momentum_ref, weights_out, momentum_out):
    momentum = decay_rate * momentum_ref[...] + grads_of(errors_ref[...], features_ref[...])
    momentum_out[...] = momentum
    weights_out[...] = weights_ref[...] - learn_rate * momentum


def encode(values, out_ref):
    rows, width = values.shape
    top = jnp.maximum(jnp.max(jnp.abs(values), axis=1, keepdims=True), SMALLEST)
    power = jnp.ceil(jnp.log(top * (1.0 / CODE_TOP)) * (1.0 / math.log(2.0)))
    codes = jnp.round(values * jnp.exp2(-power)).astype(jnp.int32)
    for j in range(width // LANES):
        out_ref[j * rows : (j + 1) * rows, :] = codes[:, j * LANES : (j + 1) * LANES].astype(jnp.int16)
    power = power.astype(jnp.int32)
    lane = lax.broadcasted_iota(jnp.int32, (TILE_ROWS, LANES), 1)
    tile = jnp.zeros((TILE_ROWS, LANES), jnp.int32)
    for g in range(rows // TILE_ROWS):
        tile = jnp.where(lane == g, power[g * TILE_ROWS : (g + 1) * TILE_ROWS, :], tile)
    out_ref[out_ref.shape[0] - TILE_ROWS :, :] = tile.astype(jnp.int16)


def decode(codes_ref, rows, width):
    tile = codes_ref[codes_ref.shape[0] - TILE_ROWS :, :].astype(jnp.float32)
    power = jnp.concatenate([tile[:, g : g + 1] for g in range(rows // TILE_ROWS)], axis=0)
    scale = jnp.exp2(power)
    return jnp.concatenate(
        [
            codes_ref[j * rows : (j + 1) * rows, :].astype(jnp.int32).astype(jnp.float32) * scale
            for j in range(width // LANES)
        ],
        axis=1,
    )


def coded_shape(rows, width):
    return jax.ShapeDtypeStruct((rows * (width // LANES) + TILE_ROWS, LANES), jnp.int16)


def fold_kernel(kept_ref, received_ref, *out_refs, coded):
    rows, width = kept_ref.shape
    total = kept_ref[...] + (decode(received_ref, rows, width) if coded else received_ref[...])
    if len(out_refs) == 2:
        out_refs[0][...] = total[: rows // 2, :]
        total = total[rows // 2 :, :]
    encode(total, out_refs[-1])


def merge_kernel(own_ref, received_ref, out_ref, *, rows, width, last):
    total = decode(own_ref, rows, width) + decode(received_ref, rows, width)
    if last:
        out_ref[...] = total
    else:
        encode(total, out_ref)


def swap(x, axis, mask):
    size = lax.axis_size(axis)
    return lax.ppermute(x, axis, [(i, i ^ mask) for i in range(size)])


def swap_by_core(x, masks):
    size = lax.axis_size("labels")
    total = lax.axis_size("rows") * size
    pairs = [(i, i ^ masks[(i // size) & 1]) for i in range(total)]
    return lax.ppermute(x, ("rows", "labels"), pairs)


def masks_of(axis):
    size = lax.axis_size(axis)
    return [1 << b for b in range(size.bit_length() - 1)]


def per_device(pool_features, pool_labels, pool_counts, batch_rows, weights, momentum):
    labels, width = weights.shape
    stored, slots = pool_labels.shape
    batches, group = batch_rows.shape
    pieces = lax.axis_size("rows")
    batch_size = pieces * group
    device_index = lax.axis_index("rows") * lax.axis_size("labels") + lax.axis_index("labels")
    base = (device_index * labels).astype(jnp.int32).reshape(1)
    vmem = pl.BlockSpec(memory_space=pltpu.VMEM)
    hbm = pl.BlockSpec(memory_space=pltpu.HBM)
    params = pltpu.CompilerParams(vmem_limit_bytes=VMEM_LIMIT)

    own = pl.pallas_call(
        select_kernel,
        out_shape=jax.ShapeDtypeStruct((batches * group, width + LANES), jnp.bfloat16),
        in_specs=[hbm] * 4,
        out_specs=vmem,
        scratch_shapes=[
            pltpu.VMEM(batch_rows.shape, jnp.int32),
            pltpu.VMEM(pool_features.shape, jnp.bfloat16),
            pltpu.VMEM((slots, stored), jnp.int32),
            pltpu.VMEM((1, stored), jnp.int32),
            pltpu.SemaphoreType.DMA((4,)),
        ],
        compiler_params=params,
        name="select_rows",
    )(*[pltpu.with_memory_space_constraint(a, pltpu.HBM) for a in (batch_rows, pool_features, pool_labels.T, pool_counts.reshape(1, stored))])

    gathered = [own]
    for mask in reversed(masks_of("rows")):
        gathered = gathered + [swap(g, "rows", mask) for g in gathered]

    weights, momentum, low_weights = pl.pallas_call(
        prepare_kernel,
        out_shape=(
            jax.ShapeDtypeStruct(weights.shape, jnp.float32),
            jax.ShapeDtypeStruct(momentum.shape, jnp.float32),
            jax.ShapeDtypeStruct(weights.shape, jnp.bfloat16),
        ),
        in_specs=[hbm, hbm, vmem],
        out_specs=(vmem,) * 3,
        scratch_shapes=[pltpu.SemaphoreType.DMA((2,))],
        compiler_params=params,
        cost_estimate=pl.CostEstimate(
            flops=0, transcendentals=0, bytes_accessed=18 * labels * width
        ),
        name="prepare",
    )(*[pltpu.with_memory_space_constraint(a, pltpu.HBM) for a in (weights, momentum)], own)

    kept, sent, errors, last, weights, momentum = pl.pallas_call(
        functools.partial(parts_kernel, pieces=pieces, group=group, slots=slots),
        out_shape=(
            jax.ShapeDtypeStruct((batches * batch_size // 2, width), jnp.float32),
            jax.ShapeDtypeStruct((batches * batch_size // 2, width), jnp.float32),
            jax.ShapeDtypeStruct((batch_size, labels), jnp.bfloat16),
            jax.ShapeDtypeStruct((batch_size, width), jnp.bfloat16),
            jax.ShapeDtypeStruct(weights.shape, jnp.float32),
            jax.ShapeDtypeStruct(momentum.shape, jnp.float32),
        ),
        in_specs=[pl.BlockSpec(memory_space=pltpu.SMEM)] + [vmem] * (pieces + 3),
        out_specs=(vmem,) * 6,
        compiler_params=params,
        name="parts",
    )(base, *gathered, weights, momentum, low_weights)

    weights, momentum = pl.pallas_call(
        update_kernel,
        out_shape=(
            jax.ShapeDtypeStruct(weights.shape, jnp.float32),
            jax.ShapeDtypeStruct(momentum.shape, jnp.float32),
        ),
        in_specs=[vmem] * 4,
        out_specs=(vmem,) * 2,
        compiler_params=params,
        cost_estimate=pl.CostEstimate(
            flops=2 * batch_size * labels * width, transcendentals=0, bytes_accessed=16 * labels * width
        ),
        name="last_update",
    )(errors, last, weights, momentum)

    received = swap(sent, "rows", 1)
    coded = False
    for mask in masks_of("rows")[1:]:
        half = kept.shape[0] // 2
        kept, sent = pl.pallas_call(
            functools.partial(fold_kernel, coded=coded),
            out_shape=(jax.ShapeDtypeStruct((half, width), jnp.float32), coded_shape(half, width)),
            in_specs=[vmem] * 2,
            out_specs=(vmem,) * 2,
            compiler_params=params,
            name="fold",
        )(kept, received)
        received = swap(sent, "rows", mask)
        coded = True
    rows = kept.shape[0]
    codes = pl.pallas_call(
        functools.partial(fold_kernel, coded=coded),
        out_shape=coded_shape(rows, width),
        in_specs=[vmem] * 2,
        out_specs=vmem,
        compiler_params=params,
        name="fold_last",
    )(kept, received)
    masks = masks_of("labels")
    for step, pair in enumerate(zip(masks, masks[1:] + masks[:1])):
        last_step = step + 1 == len(masks)
        codes = pl.pallas_call(
            functools.partial(merge_kernel, rows=rows, width=width, last=last_step),
            out_shape=jax.ShapeDtypeStruct((rows, width), jnp.float32)
            if last_step
            else coded_shape(rows, width),
            in_specs=[vmem] * 2,
            out_specs=vmem,
            compiler_params=params,
            name="merge",
        )(codes, swap_by_core(codes, pair))
    parts = codes
    return weights, momentum, parts.reshape(batches, group, width)


def solution(mesh):
    in_specs = (
        P("rows", None),
        P("rows", None),
        P("rows"),
        P(None, "rows"),
        P(("rows", "labels"), None),
        P(("rows", "labels"), None),
    )
    out_specs = (P(("rows", "labels"), None), P(("rows", "labels"), None), P(None, "rows", None))
    return jax.shard_map(
        per_device, mesh=mesh, in_specs=in_specs, out_specs=out_specs, check_vma=False
    )
```

```python
import functools
import math

import jax
import jax.numpy as jnp
from jax import lax
from jax.experimental import pallas as pl
from jax.experimental.pallas import tpu as pltpu
from jax.sharding import PartitionSpec as P

learn_rate = 0.001
decay_rate = 0.9
LANES = 128
DIGITS = 3
NO_LABEL = 255
VMEM_LIMIT = 16 << 20
TILE_ROWS = 16
CODE_TOP = 32000.0
SMALLEST = 1e-30


def fetch(sources, targets, sems):
    copies = [pltpu.make_async_copy(s, t, sems.at[i]) for i, (s, t) in enumerate(zip(sources, targets))]
    for copy in copies:
        copy.start()
    return copies


def select_kernel(rows_hbm, features_hbm, labels_hbm, counts_hbm, out_ref, rows_ref, features_ref, labels_ref, counts_ref, sems):
    copies = fetch(
        (rows_hbm, features_hbm, labels_hbm, counts_hbm), (rows_ref, features_ref, labels_ref, counts_ref), sems
    )
    for copy in copies:
        copy.wait()
    slots, stored = labels_ref.shape
    batches, group = rows_ref.shape
    width = features_ref.shape[1]
    ids = labels_ref[...]
    used = lax.broadcasted_iota(jnp.int32, (slots, stored), 0) < counts_ref[...]
    digits = [ids & 255, (ids >> 8) & 255, jnp.where(used, ids >> 16, NO_LABEL)]
    spare = LANES - DIGITS * slots
    table = jnp.concatenate(
        [d.astype(jnp.float32) for d in digits] + [jnp.zeros((spare, stored), jnp.float32)], axis=0
    ).astype(jnp.bfloat16)
    features = features_ref[...]
    for t in range(batches):
        chosen = lax.broadcasted_iota(jnp.int32, (stored, group), 0) == rows_ref[t : t + 1, :]
        one_hot = jnp.transpose(chosen.astype(jnp.float32)).astype(jnp.bfloat16)
        out_ref[t * group : (t + 1) * group, :width] = jnp.dot(
            one_hot, features, preferred_element_type=jnp.float32
        ).astype(jnp.bfloat16)
        out_ref[t * group : (t + 1) * group, width:] = lax.dot_general(
            one_hot, table, (((1,), (1,)), ((), ())), preferred_element_type=jnp.float32
        ).astype(jnp.bfloat16)


def prepare_kernel(weights_hbm, momentum_hbm, after_ref, weights_ref, decayed_ref, low_ref, sems):
    copies = fetch((weights_hbm, momentum_hbm), (weights_ref, decayed_ref), sems)
    copies[0].wait()
    low_ref[...] = weights_ref[...].astype(jnp.bfloat16)
    copies[1].wait()
    decayed_ref[...] = decay_rate * decayed_ref[...]


def batch_of(piece_refs, t, group):
    return jnp.concatenate([r[t * group : (t + 1) * group, :] for r in piece_refs], axis=0)


def features_of(piece_refs, t, group, width):
    return batch_of(piece_refs, t, group)[:, :width]


def batch_errors(features, codes, low_weights, base, slots):
    logits = lax.dot_general(
        low_weights, features, (((1,), (1,)), ((), ())), preferred_element_type=jnp.float32
    )
    labels, rows = logits.shape
    codes = jnp.transpose(codes.astype(jnp.float32))
    ids = codes[:slots, :] + 256.0 * codes[slots : 2 * slots, :] + 65536.0 * codes[2 * slots : 3 * slots, :]
    local = jnp.clip(ids - base, -1.0, float(labels)).astype(jnp.int32).astype(jnp.int16)
    label = lax.broadcasted_iota(jnp.int32, (labels, rows), 0).astype(jnp.int16)
    one, targets = jnp.ones((labels, rows), jnp.bfloat16), jnp.zeros((labels, rows), jnp.bfloat16)
    for k in range(slots):
        same = label == jnp.broadcast_to(local[k : k + 1, :], (labels, rows))
        targets = jnp.where(same, one, targets)
    return (jax.nn.sigmoid(logits) - targets.astype(jnp.float32)).astype(jnp.bfloat16)


def grads_of(errors, features):
    return jnp.dot(errors, features, preferred_element_type=jnp.float32)


def parts_kernel(base_ref, *refs, pieces, group, slots):
    piece_refs = refs[:pieces]
    weights_ref, decayed_ref, low_ref = refs[pieces : pieces + 3]
    kept_ref, sent_ref, first_ref, second_ref = refs[pieces + 3 :]
    width = weights_ref.shape[1]
    base = base_ref[0].astype(jnp.float32)

    def put(t, low_weights, errors):
        summed = lax.dot_general(
            errors, low_weights, (((0,), (0,)), ((), ())), preferred_element_type=jnp.float32
        )
        for p in range(pieces):
            half_ref = kept_ref if 2 * p < pieces else sent_ref
            start = (2 * (p % (pieces // 2)) + t) * group
            half_ref[start : start + group, :] = summed[p * group : (p + 1) * group, :]

    rows = batch_of(piece_refs, 0, group)
    features, codes = rows[:, :width], rows[:, width:]
    low_weights = low_ref[...]
    errors = batch_errors(features, codes, low_weights, base, slots)
    first_ref[...] = errors
    put(0, low_weights, errors)
    momentum = decayed_ref[...] + grads_of(errors, features)
    low_weights = (weights_ref[...] - learn_rate * momentum).astype(jnp.bfloat16)
    rows = batch_of(piece_refs, 1, group)
    features, codes = rows[:, :width], rows[:, width:]
    errors = batch_errors(features, codes, low_weights, base, slots)
    second_ref[...] = errors
    put(1, low_weights, errors)


def update_kernel(errors_ref, *refs, batch, group):
    piece_refs = refs[:-4]
    weights_ref, momentum_ref, weights_out, momentum_out = refs[-4:]
    features = features_of(piece_refs, batch, group, weights_ref.shape[1])
    momentum = momentum_ref[...] if batch == 0 else decay_rate * momentum_ref[...]
    momentum = momentum + grads_of(errors_ref[...], features)
    momentum_out[...] = momentum
    weights_out[...] = weights_ref[...] - learn_rate * momentum


def encode(values, out_ref):
    rows, width = values.shape
    top = jnp.maximum(jnp.max(jnp.abs(values), axis=1, keepdims=True), SMALLEST)
    power = jnp.ceil(jnp.log(top * (1.0 / CODE_TOP)) * (1.0 / math.log(2.0)))
    codes = jnp.round(values * jnp.exp2(-power)).astype(jnp.int32)
    for j in range(width // LANES):
        out_ref[j * rows : (j + 1) * rows, :] = codes[:, j * LANES : (j + 1) * LANES].astype(jnp.int16)
    power = power.astype(jnp.int32)
    lane = lax.broadcasted_iota(jnp.int32, (TILE_ROWS, LANES), 1)
    tile = jnp.zeros((TILE_ROWS, LANES), jnp.int32)
    for g in range(rows // TILE_ROWS):
        tile = jnp.where(lane == g, power[g * TILE_ROWS : (g + 1) * TILE_ROWS, :], tile)
    out_ref[out_ref.shape[0] - TILE_ROWS :, :] = tile.astype(jnp.int16)


def decode(codes_ref, rows, width):
    tile = codes_ref[codes_ref.shape[0] - TILE_ROWS :, :].astype(jnp.float32)
    power = jnp.concatenate([tile[:, g : g + 1] for g in range(rows // TILE_ROWS)], axis=0)
    scale = jnp.exp2(power)
    return jnp.concatenate(
        [
            codes_ref[j * rows : (j + 1) * rows, :].astype(jnp.int32).astype(jnp.float32) * scale
            for j in range(width // LANES)
        ],
        axis=1,
    )


def coded_shape(rows, width):
    return jax.ShapeDtypeStruct((rows * (width // LANES) + TILE_ROWS, LANES), jnp.int16)


def fold_kernel(kept_ref, received_ref, *out_refs, coded):
    rows, width = kept_ref.shape
    total = kept_ref[...] + (decode(received_ref, rows, width) if coded else received_ref[...])
    if len(out_refs) == 2:
        out_refs[0][...] = total[: rows // 2, :]
        total = total[rows // 2 :, :]
    encode(total, out_refs[-1])


def merge_kernel(*refs, rows, width, last):
    own, *came = [decode(r, rows, width) for r in refs[:-1]]
    total = own + came[-1]
    if len(came) == 3:
        total = total + (came[1] + came[0])
    if last:
        refs[-1][...] = total
    else:
        encode(total, refs[-1])


def swap(x, axis, mask):
    size = lax.axis_size(axis)
    return lax.ppermute(x, axis, [(i, i ^ mask) for i in range(size)])


def masks_of(axis):
    size = lax.axis_size(axis)
    return [1 << b for b in range(size.bit_length() - 1)]


def per_device(pool_features, pool_labels, pool_counts, batch_rows, weights, momentum):
    labels, width = weights.shape
    stored, slots = pool_labels.shape
    batches, group = batch_rows.shape
    pieces = lax.axis_size("rows")
    batch_size = pieces * group
    device_index = lax.axis_index("rows") * lax.axis_size("labels") + lax.axis_index("labels")
    base = (device_index * labels).astype(jnp.int32).reshape(1)
    vmem = pl.BlockSpec(memory_space=pltpu.VMEM)
    hbm = pl.BlockSpec(memory_space=pltpu.HBM)
    params = pltpu.CompilerParams(vmem_limit_bytes=VMEM_LIMIT)

    own = pl.pallas_call(
        select_kernel,
        out_shape=jax.ShapeDtypeStruct((batches * group, width + LANES), jnp.bfloat16),
        in_specs=[hbm] * 4,
        out_specs=vmem,
        scratch_shapes=[
            pltpu.VMEM(batch_rows.shape, jnp.int32),
            pltpu.VMEM(pool_features.shape, jnp.bfloat16),
            pltpu.VMEM((slots, stored), jnp.int32),
            pltpu.VMEM((1, stored), jnp.int32),
            pltpu.SemaphoreType.DMA((4,)),
        ],
        compiler_params=params,
        name="select_rows",
    )(*[pltpu.with_memory_space_constraint(a, pltpu.HBM) for a in (batch_rows, pool_features, pool_labels.T, pool_counts.reshape(1, stored))])

    weights, momentum, low_weights = pl.pallas_call(
        prepare_kernel,
        out_shape=(
            jax.ShapeDtypeStruct(weights.shape, jnp.float32),
            jax.ShapeDtypeStruct(momentum.shape, jnp.float32),
            jax.ShapeDtypeStruct(weights.shape, jnp.bfloat16),
        ),
        in_specs=[hbm, hbm, vmem],
        out_specs=(vmem,) * 3,
        scratch_shapes=[pltpu.SemaphoreType.DMA((2,))],
        compiler_params=params,
        cost_estimate=pl.CostEstimate(
            flops=0, transcendentals=0, bytes_accessed=18 * labels * width
        ),
        name="prepare",
    )(*[pltpu.with_memory_space_constraint(a, pltpu.HBM) for a in (weights, momentum)], own)

    gathered = [own]
    for mask in reversed(masks_of("rows")):
        came = [swap(g, "rows", mask) for g in gathered]
        if mask > 1:
            *came, low_weights = lax.optimization_barrier((*came, low_weights))
        gathered = gathered + came

    half = batches * batch_size // 2
    kept, sent, first, second = pl.pallas_call(
        functools.partial(parts_kernel, pieces=pieces, group=group, slots=slots),
        out_shape=(
            jax.ShapeDtypeStruct((half, width), jnp.float32),
            jax.ShapeDtypeStruct((half, width), jnp.float32),
            jax.ShapeDtypeStruct((labels, batch_size), jnp.bfloat16),
            jax.ShapeDtypeStruct((labels, batch_size), jnp.bfloat16),
        ),
        in_specs=[pl.BlockSpec(memory_space=pltpu.SMEM)] + [vmem] * (pieces + 3),
        out_specs=(vmem,) * 4,
        compiler_params=params,
        name="parts",
    )(base, *gathered, weights, momentum, low_weights)

    def update(weights, momentum):
        for batch, errors in enumerate((first, second)):
            weights, momentum = pl.pallas_call(
                functools.partial(update_kernel, batch=batch, group=group),
                out_shape=(
                    jax.ShapeDtypeStruct(weights.shape, jnp.float32),
                    jax.ShapeDtypeStruct(momentum.shape, jnp.float32),
                ),
                in_specs=[vmem] * (pieces + 3),
                out_specs=(vmem,) * 2,
                compiler_params=params,
                cost_estimate=pl.CostEstimate(
                    flops=2 * batch_size * labels * width, transcendentals=0, bytes_accessed=16 * labels * width
                ),
                name=f"update_{batch}",
            )(errors, *gathered, weights, momentum)
        return weights, momentum

    received = swap(sent, "rows", 1)
    coded = False
    for mask in masks_of("rows")[1:]:
        half = kept.shape[0] // 2
        kept, sent = pl.pallas_call(
            functools.partial(fold_kernel, coded=coded),
            out_shape=(jax.ShapeDtypeStruct((half, width), jnp.float32), coded_shape(half, width)),
            in_specs=[vmem] * 2,
            out_specs=(vmem,) * 2,
            compiler_params=params,
            name="fold",
        )(kept, received)
        received = swap(sent, "rows", mask)
        if not coded:
            received, weights, momentum = lax.optimization_barrier((received, *update(weights, momentum)))
        coded = True
    rows = kept.shape[0]
    codes = pl.pallas_call(
        functools.partial(fold_kernel, coded=coded),
        out_shape=coded_shape(rows, width),
        in_specs=[vmem] * 2,
        out_specs=vmem,
        compiler_params=params,
        name="fold_last",
    )(kept, received)
    masks = masks_of("labels")
    steps = [masks[i : i + 2] for i in range(0, len(masks), 2)]
    for step in steps:
        last = step is steps[-1]
        partners = [step[0]] if len(step) == 1 else [step[0], step[1], step[0] | step[1]]
        came = [swap(codes, "labels", mask) for mask in reversed(partners)]
        codes = pl.pallas_call(
            functools.partial(merge_kernel, rows=rows, width=width, last=last),
            out_shape=jax.ShapeDtypeStruct((rows, width), jnp.float32)
            if last
            else coded_shape(rows, width),
            in_specs=[vmem] * (1 + len(came)),
            out_specs=vmem,
            compiler_params=params,
            name="merge",
        )(codes, *came)
    parts = codes
    return weights, momentum, parts.reshape(batches, group, width)


def solution(mesh):
    in_specs = (
        P("rows", None),
        P("rows", None),
        P("rows"),
        P(None, "rows"),
        P(("rows", "labels"), None),
        P(("rows", "labels"), None),
    )
    out_specs = (P(("rows", "labels"), None), P(("rows", "labels"), None), P(None, "rows", None))
    return jax.shard_map(
        per_device, mesh=mesh, in_specs=in_specs, out_specs=out_specs, check_vma=False
    )
```

```python
import functools
import math

import jax
import jax.numpy as jnp
from jax import lax
from jax.experimental import pallas as pl
from jax.experimental.pallas import tpu as pltpu
from jax.sharding import PartitionSpec as P

learn_rate = 0.001
decay_rate = 0.9
LANES = 128
DIGITS = 3
NO_LABEL = 255
VMEM_LIMIT = 16 << 20
COLUMNS = 256
TILE_ROWS = 16
CODE_TOP = 32000.0
SMALLEST = 1e-30


def fetch(sources, targets, sems):
    copies = [pltpu.make_async_copy(s, t, sems.at[i]) for i, (s, t) in enumerate(zip(sources, targets))]
    for copy in copies:
        copy.start()
    return copies


def select_kernel(rows_hbm, features_hbm, labels_hbm, counts_hbm, out_ref, rows_ref, features_ref, labels_ref, counts_ref, sems):
    copies = fetch(
        (rows_hbm, features_hbm, labels_hbm, counts_hbm), (rows_ref, features_ref, labels_ref, counts_ref), sems
    )
    for copy in copies:
        copy.wait()
    slots, stored = labels_ref.shape
    batches, group = rows_ref.shape
    width = features_ref.shape[1]
    ids = labels_ref[...]
    used = lax.broadcasted_iota(jnp.int32, (slots, stored), 0) < counts_ref[...]
    digits = [ids & 255, (ids >> 8) & 255, jnp.where(used, ids >> 16, NO_LABEL)]
    spare = LANES - DIGITS * slots
    table = jnp.concatenate(
        [d.astype(jnp.float32) for d in digits] + [jnp.zeros((spare, stored), jnp.float32)], axis=0
    ).astype(jnp.bfloat16)
    one_hot = jnp.concatenate(
        [
            jnp.transpose(
                jnp.where(
                    lax.broadcasted_iota(jnp.int32, (stored, group), 0) == rows_ref[t : t + 1, :], 1.0, 0.0
                )
            )
            for t in range(batches)
        ],
        axis=0,
    ).astype(jnp.bfloat16)
    out_ref[:, :width] = jnp.dot(one_hot, features_ref[...], preferred_element_type=jnp.float32).astype(jnp.bfloat16)
    out_ref[:, width:] = lax.dot_general(
        one_hot, table, (((1,), (1,)), ((), ())), preferred_element_type=jnp.float32
    ).astype(jnp.bfloat16)


def prepare_kernel(weights_hbm, momentum_hbm, after_ref, weights_ref, decayed_ref, low_ref, sems):
    copies = fetch((weights_hbm, momentum_hbm), (weights_ref, decayed_ref), sems)
    copies[0].wait()
    low_ref[...] = weights_ref[...].astype(jnp.bfloat16)
    copies[1].wait()
    decayed_ref[...] = decay_rate * decayed_ref[...]


def batch_of(piece_refs, t, group):
    return jnp.concatenate([r[t * group : (t + 1) * group, :] for r in piece_refs], axis=0)


def features_of(piece_refs, t, group, width):
    return batch_of(piece_refs, t, group)[:, :width]


def targets_of(codes, labels, base, slots):
    rows = codes.shape[0]
    codes = jnp.transpose(codes.astype(jnp.float32))
    ids = codes[:slots, :] + 256.0 * codes[slots : 2 * slots, :] + 65536.0 * codes[2 * slots : 3 * slots, :]
    local = jnp.clip(ids - base, -1.0, float(labels)).astype(jnp.int32).astype(jnp.int16)
    label = lax.broadcasted_iota(jnp.int32, (labels, rows), 0).astype(jnp.int16)
    one, targets = jnp.ones((labels, rows), jnp.bfloat16), jnp.zeros((labels, rows), jnp.bfloat16)
    for k in range(slots):
        same = label == jnp.broadcast_to(local[k : k + 1, :], (labels, rows))
        targets = jnp.where(same, one, targets)
    return targets


def across(a, b):
    return lax.dot_general(a, b, (((1,), (1,)), ((), ())), preferred_element_type=jnp.float32)


def errors_of(logits, targets):
    return (jax.nn.sigmoid(logits) - targets.astype(jnp.float32)).astype(jnp.bfloat16)


def grads_of(errors, features):
    return jnp.dot(errors, features, preferred_element_type=jnp.float32)


def parts_kernel(base_ref, *refs, pieces, group, slots):
    piece_refs = refs[:pieces]
    weights_ref, decayed_ref, low_ref = refs[pieces : pieces + 3]
    kept_ref, sent_ref, first_ref, second_ref, targets_ref = refs[pieces + 3 :]
    labels, width = weights_ref.shape
    half = labels // 2
    base = base_ref[0].astype(jnp.float32)
    chunks = [slice(c, min(c + COLUMNS, width)) for c in range(0, width, COLUMNS)]

    def put(t, errors, low_weights):
        for c, low in zip(chunks, low_weights):
            summed = lax.dot_general(
                errors, low, (((0,), (0,)), ((), ())), preferred_element_type=jnp.float32
            )
            for p in range(pieces):
                half_ref = kept_ref if 2 * p < pieces else sent_ref
                start = (2 * (p % (pieces // 2)) + t) * group
                half_ref[start : start + group, c] = summed[p * group : (p + 1) * group, :]

    rows = batch_of(piece_refs, 0, group)
    features = rows[:, :width]
    logits = [across(low_ref[i * half : (i + 1) * half, :], features) for i in range(2)]
    targets = targets_of(rows[:, width:], labels, base, slots)
    errors = errors_of(jnp.concatenate(logits, axis=0), targets)
    first_ref[...] = errors
    next_rows = batch_of(piece_refs, 1, group)
    targets_ref[...] = targets_of(next_rows[:, width:], labels, base, slots)
    next_low, logits = [], 0.0
    for c in chunks:
        momentum = decayed_ref[:, c] + grads_of(errors, features[:, c])
        low = (weights_ref[:, c] - learn_rate * momentum).astype(jnp.bfloat16)
        next_low.append(low)
        logits = logits + across(low, next_rows[:, c])
    put(0, errors, [low_ref[:, c] for c in chunks])
    errors = errors_of(logits, targets_ref[...])
    second_ref[...] = errors
    put(1, errors, next_low)


def update_kernel(errors_ref, *refs, batch, group):
    piece_refs = refs[:-4]
    weights_ref, momentum_ref, weights_out, momentum_out = refs[-4:]
    features = features_of(piece_refs, batch, group, weights_ref.shape[1])
    momentum = momentum_ref[...] if batch == 0 else decay_rate * momentum_ref[...]
    momentum = momentum + grads_of(errors_ref[...], features)
    momentum_out[...] = momentum
    weights_out[...] = weights_ref[...] - learn_rate * momentum


def encode(blocks, out_ref):
    rows = TILE_ROWS * len(blocks)
    lane = lax.broadcasted_iota(jnp.int32, (TILE_ROWS, LANES), 1)
    tile = jnp.zeros((TILE_ROWS, LANES), jnp.float32)
    for g, values in enumerate(blocks):
        top = jnp.maximum(jnp.max(jnp.abs(values), axis=1, keepdims=True), SMALLEST)
        power = jnp.ceil(jnp.log(top * (1.0 / CODE_TOP)) * (1.0 / math.log(2.0)))
        codes = jnp.round(values * jnp.exp2(-power)).astype(jnp.int32).astype(jnp.int16)
        for j in range(values.shape[1] // LANES):
            start = j * rows + g * TILE_ROWS
            out_ref[start : start + TILE_ROWS, :] = codes[:, j * LANES : (j + 1) * LANES]
        tile = jnp.where(lane == g, power, tile)
    out_ref[out_ref.shape[0] - TILE_ROWS :, :] = tile.astype(jnp.int32).astype(jnp.int16)


def decode(codes_ref, g, rows, width):
    scale = jnp.exp2(codes_ref[codes_ref.shape[0] - TILE_ROWS :, :].astype(jnp.float32)[:, g : g + 1])
    start = g * TILE_ROWS
    return jnp.concatenate(
        [
            codes_ref[j * rows + start : j * rows + start + TILE_ROWS, :].astype(jnp.float32) * scale
            for j in range(width // LANES)
        ],
        axis=1,
    )


def coded_shape(rows, width):
    return jax.ShapeDtypeStruct((rows * (width // LANES) + TILE_ROWS, LANES), jnp.int16)


def fold_kernel(kept_ref, received_ref, *out_refs, coded):
    rows, width = kept_ref.shape
    blocks = []
    for g in range(rows // TILE_ROWS):
        at = slice(g * TILE_ROWS, (g + 1) * TILE_ROWS)
        total = kept_ref[at, :] + (decode(received_ref, g, rows, width) if coded else received_ref[at, :])
        if len(out_refs) == 2 and at.stop <= rows // 2:
            out_refs[0][at, :] = total
        else:
            blocks.append(total)
    encode(blocks, out_refs[-1])


def merged(refs, g, rows, width):
    own, *came = [decode(r, g, rows, width) for r in refs]
    total = own + came[-1]
    if len(came) == 3:
        total = total + (came[1] + came[0])
    return total


def merge_kernel(*refs, rows, width):
    encode([merged(refs[:-1], g, rows, width) for g in range(rows // TILE_ROWS)], refs[-1])


def last_merge_kernel(*refs, rows, width):
    *came, out_hbm, out_ref, sems = refs
    copies = []
    for g in range(rows // TILE_ROWS):
        at = pl.ds(g * TILE_ROWS, TILE_ROWS)
        out_ref[at, :] = merged(came, g, rows, width)
        copies.append(pltpu.make_async_copy(out_ref.at[at], out_hbm.at[at], sems.at[g]))
        copies[-1].start()
    for copy in copies:
        copy.wait()


def swap(x, axis, mask):
    size = lax.axis_size(axis)
    return lax.ppermute(x, axis, [(i, i ^ mask) for i in range(size)])


def masks_of(axis):
    size = lax.axis_size(axis)
    return [1 << b for b in range(size.bit_length() - 1)]


def per_device(pool_features, pool_labels, pool_counts, batch_rows, weights, momentum):
    labels, width = weights.shape
    stored, slots = pool_labels.shape
    batches, group = batch_rows.shape
    pieces = lax.axis_size("rows")
    batch_size = pieces * group
    device_index = lax.axis_index("rows") * lax.axis_size("labels") + lax.axis_index("labels")
    base = (device_index * labels).astype(jnp.int32).reshape(1)
    vmem = pl.BlockSpec(memory_space=pltpu.VMEM)
    hbm = pl.BlockSpec(memory_space=pltpu.HBM)
    params = pltpu.CompilerParams(vmem_limit_bytes=VMEM_LIMIT)

    own = pl.pallas_call(
        select_kernel,
        out_shape=jax.ShapeDtypeStruct((batches * group, width + LANES), jnp.bfloat16),
        in_specs=[hbm] * 4,
        out_specs=vmem,
        scratch_shapes=[
            pltpu.VMEM(batch_rows.shape, jnp.int32),
            pltpu.VMEM(pool_features.shape, jnp.bfloat16),
            pltpu.VMEM((slots, stored), jnp.int32),
            pltpu.VMEM((1, stored), jnp.int32),
            pltpu.SemaphoreType.DMA((4,)),
        ],
        compiler_params=params,
        name="select_rows",
    )(*[pltpu.with_memory_space_constraint(a, pltpu.HBM) for a in (batch_rows, pool_features, pool_labels.T, pool_counts.reshape(1, stored))])

    weights, momentum, low_weights = pl.pallas_call(
        prepare_kernel,
        out_shape=(
            jax.ShapeDtypeStruct(weights.shape, jnp.float32),
            jax.ShapeDtypeStruct(momentum.shape, jnp.float32),
            jax.ShapeDtypeStruct(weights.shape, jnp.bfloat16),
        ),
        in_specs=[hbm, hbm, vmem],
        out_specs=(vmem,) * 3,
        scratch_shapes=[pltpu.SemaphoreType.DMA((2,))],
        compiler_params=params,
        cost_estimate=pl.CostEstimate(
            flops=0, transcendentals=0, bytes_accessed=18 * labels * width
        ),
        name="prepare",
    )(*[pltpu.with_memory_space_constraint(a, pltpu.HBM) for a in (weights, momentum)], own)

    gathered = [own]
    for mask in reversed(masks_of("rows")):
        came = [swap(g, "rows", mask) for g in gathered]
        if mask > 1:
            *came, low_weights = lax.optimization_barrier((*came, low_weights))
        gathered = gathered + came

    half = batches * batch_size // 2
    kept, sent, first, second = pl.pallas_call(
        functools.partial(parts_kernel, pieces=pieces, group=group, slots=slots),
        out_shape=(
            jax.ShapeDtypeStruct((half, width), jnp.float32),
            jax.ShapeDtypeStruct((half, width), jnp.float32),
            jax.ShapeDtypeStruct((labels, batch_size), jnp.bfloat16),
            jax.ShapeDtypeStruct((labels, batch_size), jnp.bfloat16),
        ),
        in_specs=[pl.BlockSpec(memory_space=pltpu.SMEM)] + [vmem] * (pieces + 3),
        out_specs=(vmem,) * 4,
        scratch_shapes=[pltpu.VMEM((labels, batch_size), jnp.bfloat16)],
        compiler_params=params,
        name="parts",
    )(base, *gathered, weights, momentum, low_weights)

    def update(weights, momentum):
        for batch, errors in enumerate((first, second)):
            weights, momentum = pl.pallas_call(
                functools.partial(update_kernel, batch=batch, group=group),
                out_shape=(
                    jax.ShapeDtypeStruct(weights.shape, jnp.float32),
                    jax.ShapeDtypeStruct(momentum.shape, jnp.float32),
                ),
                in_specs=[vmem] * (pieces + 3),
                out_specs=(vmem,) * 2,
                compiler_params=params,
                cost_estimate=pl.CostEstimate(
                    flops=2 * batch_size * labels * width, transcendentals=0, bytes_accessed=16 * labels * width
                ),
                name=f"update_{batch}",
            )(errors, *gathered, weights, momentum)
        return weights, momentum

    received = swap(sent, "rows", 1)
    coded = False
    for mask in masks_of("rows")[1:]:
        half = kept.shape[0] // 2
        kept, sent = pl.pallas_call(
            functools.partial(fold_kernel, coded=coded),
            out_shape=(jax.ShapeDtypeStruct((half, width), jnp.float32), coded_shape(half, width)),
            in_specs=[vmem] * 2,
            out_specs=(vmem,) * 2,
            compiler_params=params,
            name="fold",
        )(kept, received)
        received = swap(sent, "rows", mask)
        if not coded:
            received, weights, momentum = lax.optimization_barrier((received, *update(weights, momentum)))
        coded = True
    rows = kept.shape[0]
    codes = pl.pallas_call(
        functools.partial(fold_kernel, coded=coded),
        out_shape=coded_shape(rows, width),
        in_specs=[vmem] * 2,
        out_specs=vmem,
        compiler_params=params,
        name="fold_last",
    )(kept, received)
    masks = masks_of("labels")
    steps = [masks[i : i + 2] for i in range(0, len(masks), 2)]
    for step in steps:
        partners = [step[0]] if len(step) == 1 else [step[0], step[1], step[0] | step[1]]
        came = [swap(codes, "labels", mask) for mask in reversed(partners)]
        if step is not steps[-1]:
            codes = pl.pallas_call(
                functools.partial(merge_kernel, rows=rows, width=width),
                out_shape=coded_shape(rows, width),
                in_specs=[vmem] * (1 + len(came)),
                out_specs=vmem,
                compiler_params=params,
                name="merge",
            )(codes, *came)
    parts = pl.pallas_call(
        functools.partial(last_merge_kernel, rows=rows, width=width),
        out_shape=jax.ShapeDtypeStruct((rows, width), jnp.float32),
        in_specs=[vmem] * (1 + len(came)),
        out_specs=hbm,
        scratch_shapes=[
            pltpu.VMEM((rows, width), jnp.float32),
            pltpu.SemaphoreType.DMA((rows // TILE_ROWS,)),
        ],
        compiler_params=params,
        name="last_merge",
    )(codes, *came)
    return weights, momentum, parts.reshape(batches, group, width)


def solution(mesh):
    in_specs = (
        P("rows", None),
        P("rows", None),
        P("rows"),
        P(None, "rows"),
        P(("rows", "labels"), None),
        P(("rows", "labels"), None),
    )
    out_specs = (P(("rows", "labels"), None), P(("rows", "labels"), None), P(None, "rows", None))
    return jax.shard_map(
        per_device, mesh=mesh, in_specs=in_specs, out_specs=out_specs, check_vma=False
    )
```

```python
import functools
import math

import jax
import jax.numpy as jnp
from jax import lax
from jax.experimental import pallas as pl
from jax.experimental.pallas import tpu as pltpu
from jax.sharding import PartitionSpec as P

learn_rate = 0.001
decay_rate = 0.9
LANES = 128
NO_LABEL = 255
VMEM_LIMIT = 16 << 20
COLUMNS = 256
PARTS = 4
TILE_ROWS = 16
CODE_TOP = 32000.0
SMALLEST = 1e-30


def fetch(sources, targets, sems):
    copies = [pltpu.make_async_copy(s, t, sems.at[i]) for i, (s, t) in enumerate(zip(sources, targets))]
    for copy in copies:
        copy.start()
    return copies


def select_kernel(
    rows_hbm,
    features_hbm,
    labels_hbm,
    counts_hbm,
    out_ref,
    rows_ref,
    features_ref,
    labels_ref,
    counts_ref,
    sems,
    *,
    digits,
):
    slots, stored = labels_ref.shape
    batches, group = rows_ref.shape
    width = features_ref.shape[1]
    part = stored // PARTS
    bands = [pl.ds(i * part, part) for i in range(PARTS)]
    copies = fetch(
        (rows_hbm, labels_hbm, counts_hbm, *[features_hbm.at[band] for band in bands]),
        (rows_ref, labels_ref, counts_ref, *[features_ref.at[band] for band in bands]),
        sems,
    )
    copies[0].wait()
    rows = batches * group
    one_hot = jnp.concatenate(
        [
            jnp.transpose(
                jnp.where(
                    lax.broadcasted_iota(jnp.int32, (stored, group), 0) == rows_ref[t : t + 1, :], 1.0, 0.0
                )
            )
            for t in range(batches)
        ],
        axis=0,
    ).astype(jnp.bfloat16)
    for copy in copies[1:]:
        copy.wait()
    ids = labels_ref[...]
    used = lax.broadcasted_iota(jnp.int32, (slots, stored), 0) < counts_ref[...]
    table = [(ids >> (8 * i)) & 255 for i in range(digits - 1)]
    table.append(jnp.where(used, ids >> (8 * (digits - 1)), NO_LABEL))
    table = jnp.concatenate(table, axis=0).astype(jnp.float32).astype(jnp.bfloat16)
    codes = across(table, one_hot)
    codes = [codes[i * slots : (i + 1) * slots, :] for i in range(digits)]
    codes += [jnp.zeros((slots, rows), jnp.float32)] * (digits % 2)
    start = rows * (width // LANES)
    for i in range(0, digits, 2):
        out_ref[start : start + slots, :] = jnp.concatenate(codes[i : i + 2], axis=1).astype(jnp.bfloat16)
        start += slots
    chosen = jnp.dot(one_hot, features_ref[...], preferred_element_type=jnp.float32).astype(jnp.bfloat16)
    for j in range(width // LANES):
        out_ref[j * rows : (j + 1) * rows, :] = chosen[:, j * LANES : (j + 1) * LANES]


def prepare_kernel(weights_hbm, momentum_hbm, after_ref, weights_ref, decayed_ref, low_ref, sems):
    copies = fetch((weights_hbm, momentum_hbm), (weights_ref, decayed_ref), sems)
    copies[0].wait()
    low_ref[...] = weights_ref[...].astype(jnp.bfloat16)
    copies[1].wait()
    decayed_ref[...] = decay_rate * decayed_ref[...]


def features_of(piece_refs, batch, batches, group, width):
    rows = batches * group
    starts = [j * rows + batch * group for j in range(width // LANES)]
    return jnp.concatenate(
        [jnp.concatenate([r[i : i + group, :] for r in piece_refs], axis=0) for i in starts], axis=1
    )


def ids_of(piece_refs, batches, group, width, slots, digits):
    rows = batches * group
    start = rows * (width // LANES)
    ids = []
    for r in piece_refs:
        total = 0.0
        for i in range(digits):
            at = start + slots * (i // 2)
            total = total + 256.0**i * r[at : at + slots, :].astype(jnp.float32)[:, rows * (i % 2) : rows * (i % 2 + 1)]
        ids.append(total)
    return [jnp.concatenate([t[:, b * group : (b + 1) * group] for t in ids], axis=1) for b in range(batches)]


def targets_of(ids, labels, base):
    slots, rows = ids.shape
    local = jnp.clip(ids - base, -1.0, float(labels)).astype(jnp.int32).astype(jnp.int16)
    label = lax.broadcasted_iota(jnp.int32, (labels, rows), 0).astype(jnp.int16)
    one, targets = jnp.ones((labels, rows), jnp.bfloat16), jnp.zeros((labels, rows), jnp.bfloat16)
    for k in range(slots):
        same = label == jnp.broadcast_to(local[k : k + 1, :], (labels, rows))
        targets = jnp.where(same, one, targets)
    return targets


def across(a, b):
    return lax.dot_general(a, b, (((1,), (1,)), ((), ())), preferred_element_type=jnp.float32)


def errors_of(logits, targets):
    return (jax.nn.sigmoid(logits) - targets.astype(jnp.float32)).astype(jnp.bfloat16)


def grads_of(errors, features):
    return jnp.dot(errors, features, preferred_element_type=jnp.float32)


def parts_kernel(base_ref, *refs, pieces, batches, group, slots, digits):
    piece_refs = refs[:pieces]
    weights_ref, decayed_ref, low_ref = refs[pieces : pieces + 3]
    *part_refs, first_ref, second_ref, targets_ref = refs[pieces + 3 :]
    share = pieces // len(part_refs)
    labels, width = weights_ref.shape
    half = labels // 2
    base = base_ref[0].astype(jnp.float32)
    chunks = [slice(c, min(c + COLUMNS, width)) for c in range(0, width, COLUMNS)]

    def put(t, errors, low_weights):
        for c, low in zip(chunks, low_weights):
            summed = lax.dot_general(
                errors, low, (((0,), (0,)), ((), ())), preferred_element_type=jnp.float32
            )
            for p in range(pieces):
                start = (2 * (p % share) + t) * group
                part_refs[p // share][start : start + group, c] = summed[p * group : (p + 1) * group, :]

    ids = ids_of(piece_refs, batches, group, width, slots, digits)
    features = features_of(piece_refs, 0, batches, group, width)
    logits = [across(low_ref[i * half : (i + 1) * half, :], features) for i in range(2)]
    targets = targets_of(ids[0], labels, base)
    errors = errors_of(jnp.concatenate(logits, axis=0), targets)
    first_ref[...] = errors
    next_features = features_of(piece_refs, 1, batches, group, width)
    targets_ref[...] = targets_of(ids[1], labels, base)
    next_low, logits = [], 0.0
    for c in chunks:
        momentum = decayed_ref[:, c] + grads_of(errors, features[:, c])
        low = (weights_ref[:, c] - learn_rate * momentum).astype(jnp.bfloat16)
        next_low.append(low)
        logits = logits + across(low, next_features[:, c])
    put(0, errors, [low_ref[:, c] for c in chunks])
    errors = errors_of(logits, targets_ref[...])
    second_ref[...] = errors
    put(1, errors, next_low)


def update_kernel(errors_ref, *refs, batch, batches, group):
    piece_refs = refs[:-4]
    weights_ref, momentum_ref, weights_out, momentum_out = refs[-4:]
    features = features_of(piece_refs, batch, batches, group, weights_ref.shape[1])
    momentum = momentum_ref[...] if batch == 0 else decay_rate * momentum_ref[...]
    momentum = momentum + grads_of(errors_ref[...], features)
    momentum_out[...] = momentum
    weights_out[...] = weights_ref[...] - learn_rate * momentum


def encode(blocks, out_ref):
    rows = TILE_ROWS * len(blocks)
    lane = lax.broadcasted_iota(jnp.int32, (TILE_ROWS, LANES), 1)
    tile = jnp.zeros((TILE_ROWS, LANES), jnp.float32)
    for g, values in enumerate(blocks):
        top = jnp.maximum(jnp.max(jnp.abs(values), axis=1, keepdims=True), SMALLEST)
        power = jnp.ceil(jnp.log(top * (1.0 / CODE_TOP)) * (1.0 / math.log(2.0)))
        codes = jnp.round(values * jnp.exp2(-power)).astype(jnp.int32).astype(jnp.int16)
        for j in range(values.shape[1] // LANES):
            start = j * rows + g * TILE_ROWS
            out_ref[start : start + TILE_ROWS, :] = codes[:, j * LANES : (j + 1) * LANES]
        tile = jnp.where(lane == g, power, tile)
    out_ref[out_ref.shape[0] - TILE_ROWS :, :] = tile.astype(jnp.int32).astype(jnp.int16)


def decode(codes_ref, g, rows, width):
    scale = jnp.exp2(codes_ref[codes_ref.shape[0] - TILE_ROWS :, :].astype(jnp.float32)[:, g : g + 1])
    start = g * TILE_ROWS
    return jnp.concatenate(
        [
            codes_ref[j * rows + start : j * rows + start + TILE_ROWS, :].astype(jnp.float32) * scale
            for j in range(width // LANES)
        ],
        axis=1,
    )


def coded_shape(rows, width):
    return jax.ShapeDtypeStruct((rows * (width // LANES) + TILE_ROWS, LANES), jnp.int16)


def fold_kernel(kept_ref, received_ref, *out_refs, coded):
    rows, width = kept_ref.shape
    blocks = []
    for g in range(rows // TILE_ROWS):
        at = slice(g * TILE_ROWS, (g + 1) * TILE_ROWS)
        total = kept_ref[at, :] + (decode(received_ref, g, rows, width) if coded else received_ref[at, :])
        if len(out_refs) == 2 and at.stop <= rows // 2:
            out_refs[0][at, :] = total
        else:
            blocks.append(total)
    encode(blocks, out_refs[-1])


def merged(refs, g, rows, width):
    own, *came = [decode(r, g, rows, width) for r in refs]
    total = own + came[-1]
    if len(came) == 3:
        total = total + (came[1] + came[0])
    return total


def merge_kernel(*refs, rows, width):
    encode([merged(refs[:-1], g, rows, width) for g in range(rows // TILE_ROWS)], refs[-1])


def last_merge_kernel(*refs, rows, width):
    *came, out_hbm, out_ref, sems = refs
    copies = []
    for g in range(rows // TILE_ROWS):
        at = pl.ds(g * TILE_ROWS, TILE_ROWS)
        out_ref[at, :] = merged(came, g, rows, width)
        copies.append(pltpu.make_async_copy(out_ref.at[at], out_hbm.at[at], sems.at[g]))
        copies[-1].start()
    for copy in copies:
        copy.wait()


def swap(x, axis, mask):
    size = lax.axis_size(axis)
    return lax.ppermute(x, axis, [(i, i ^ mask) for i in range(size)])


def masks_of(axis):
    size = lax.axis_size(axis)
    return [1 << b for b in range(size.bit_length() - 1)]


def per_device(pool_features, pool_labels, pool_counts, batch_rows, weights, momentum):
    labels, width = weights.shape
    stored, slots = pool_labels.shape
    batches, group = batch_rows.shape
    pieces = lax.axis_size("rows")
    batch_size = pieces * group
    digits = 2 if pieces * lax.axis_size("labels") * labels <= NO_LABEL * 256 else 3
    device_index = lax.axis_index("rows") * lax.axis_size("labels") + lax.axis_index("labels")
    base = (device_index * labels).astype(jnp.int32).reshape(1)
    vmem = pl.BlockSpec(memory_space=pltpu.VMEM)
    hbm = pl.BlockSpec(memory_space=pltpu.HBM)
    params = pltpu.CompilerParams(vmem_limit_bytes=VMEM_LIMIT)

    own = pl.pallas_call(
        functools.partial(select_kernel, digits=digits),
        out_shape=jax.ShapeDtypeStruct(
            (batches * group * (width // LANES) + slots * ((digits + 1) // 2), LANES), jnp.bfloat16
        ),
        in_specs=[hbm] * 4,
        out_specs=vmem,
        scratch_shapes=[
            pltpu.VMEM(batch_rows.shape, jnp.int32),
            pltpu.VMEM(pool_features.shape, jnp.bfloat16),
            pltpu.VMEM((slots, stored), jnp.int32),
            pltpu.VMEM((1, stored), jnp.int32),
            pltpu.SemaphoreType.DMA((3 + PARTS,)),
        ],
        compiler_params=params,
        name="select_rows",
    )(*[pltpu.with_memory_space_constraint(a, pltpu.HBM) for a in (batch_rows, pool_features, pool_labels.T, pool_counts.reshape(1, stored))])

    weights, momentum, low_weights = pl.pallas_call(
        prepare_kernel,
        out_shape=(
            jax.ShapeDtypeStruct(weights.shape, jnp.float32),
            jax.ShapeDtypeStruct(momentum.shape, jnp.float32),
            jax.ShapeDtypeStruct(weights.shape, jnp.bfloat16),
        ),
        in_specs=[hbm, hbm, vmem],
        out_specs=(vmem,) * 3,
        scratch_shapes=[pltpu.SemaphoreType.DMA((2,))],
        compiler_params=params,
        cost_estimate=pl.CostEstimate(
            flops=0, transcendentals=0, bytes_accessed=18 * labels * width
        ),
        name="prepare",
    )(*[pltpu.with_memory_space_constraint(a, pltpu.HBM) for a in (weights, momentum)], own)

    gathered = [own]
    for mask in reversed(masks_of("rows")):
        came = [swap(g, "rows", mask) for g in gathered]
        if mask > 1:
            *came, low_weights = lax.optimization_barrier((*came, low_weights))
        gathered = gathered + came

    quarter = batches * batch_size // 4
    kept, moved, kept_theirs, moved_theirs, first, second = pl.pallas_call(
        functools.partial(
            parts_kernel, pieces=pieces, batches=batches, group=group, slots=slots, digits=digits
        ),
        out_shape=(
            *[jax.ShapeDtypeStruct((quarter, width), jnp.float32)] * 4,
            jax.ShapeDtypeStruct((labels, batch_size), jnp.bfloat16),
            jax.ShapeDtypeStruct((labels, batch_size), jnp.bfloat16),
        ),
        in_specs=[pl.BlockSpec(memory_space=pltpu.SMEM)] + [vmem] * (pieces + 3),
        out_specs=(vmem,) * 6,
        scratch_shapes=[pltpu.VMEM((labels, batch_size), jnp.bfloat16)],
        compiler_params=params,
        name="parts",
    )(base, *gathered, weights, momentum, low_weights)

    def update(weights, momentum):
        for batch, errors in enumerate((first, second)):
            weights, momentum = pl.pallas_call(
                functools.partial(update_kernel, batch=batch, batches=batches, group=group),
                out_shape=(
                    jax.ShapeDtypeStruct(weights.shape, jnp.float32),
                    jax.ShapeDtypeStruct(momentum.shape, jnp.float32),
                ),
                in_specs=[vmem] * (pieces + 3),
                out_specs=(vmem,) * 2,
                compiler_params=params,
                cost_estimate=pl.CostEstimate(
                    flops=2 * batch_size * labels * width, transcendentals=0, bytes_accessed=16 * labels * width
                ),
                name=f"update_{batch}",
            )(errors, *gathered, weights, momentum)
        return weights, momentum

    def add(a, b, halve):
        rows = a.shape[0] // 2 if halve else a.shape[0]
        out = coded_shape(rows, width)
        return pl.pallas_call(
            functools.partial(fold_kernel, coded=b.dtype == jnp.int16),
            out_shape=(jax.ShapeDtypeStruct((rows, width), jnp.float32), out) if halve else out,
            in_specs=[vmem] * 2,
            out_specs=(vmem,) * 2 if halve else vmem,
            compiler_params=params,
            name="fold",
        )(a, b)

    masks = masks_of("rows")[1:]
    codes = add(moved, swap(moved_theirs, "rows", 1), False)
    received = swap(codes, "rows", masks[0])
    kept = kept + swap(kept_theirs, "rows", 1)
    received, kept, weights, momentum = lax.optimization_barrier((received, kept, *update(weights, momentum)))
    for mask in masks[1:]:
        kept, codes = add(kept, received, True)
        received = swap(codes, "rows", mask)
    rows = kept.shape[0]
    codes = add(kept, received, False)
    masks = masks_of("labels")
    steps = [masks[i : i + 2] for i in range(0, len(masks), 2)]
    for step in steps:
        partners = [step[0]] if len(step) == 1 else [step[0], step[1], step[0] | step[1]]
        came = [swap(codes, "labels", mask) for mask in reversed(partners)]
        if step is not steps[-1]:
            codes = pl.pallas_call(
                functools.partial(merge_kernel, rows=rows, width=width),
                out_shape=coded_shape(rows, width),
                in_specs=[vmem] * (1 + len(came)),
                out_specs=vmem,
                compiler_params=params,
                name="merge",
            )(codes, *came)
    parts = pl.pallas_call(
        functools.partial(last_merge_kernel, rows=rows, width=width),
        out_shape=jax.ShapeDtypeStruct((rows, width), jnp.float32),
        in_specs=[vmem] * (1 + len(came)),
        out_specs=hbm,
        scratch_shapes=[
            pltpu.VMEM((rows, width), jnp.float32),
            pltpu.SemaphoreType.DMA((rows // TILE_ROWS,)),
        ],
        compiler_params=params,
        name="last_merge",
    )(codes, *came)
    return weights, momentum, parts.reshape(batches, group, width)


def solution(mesh):
    in_specs = (
        P("rows", None),
        P("rows", None),
        P("rows"),
        P(None, "rows"),
        P(("rows", "labels"), None),
        P(("rows", "labels"), None),
    )
    out_specs = (P(("rows", "labels"), None), P(("rows", "labels"), None), P(None, "rows", None))
    return jax.shard_map(
        per_device, mesh=mesh, in_specs=in_specs, out_specs=out_specs, check_vma=False
    )
```

```python
import functools
import math

import jax
import jax.numpy as jnp
from jax import lax
from jax.experimental import pallas as pl
from jax.experimental.pallas import tpu as pltpu
from jax.sharding import PartitionSpec as P

learn_rate = 0.001
decay_rate = 0.9
LANES = 128
NO_LABEL = 255
VMEM_LIMIT = 16 << 20
COLUMNS = 256
PARTS = 4
TILE_ROWS = 16
CODE_TOP = 32000.0
SMALLEST = 1e-30


def fetch(sources, targets, sems):
    copies = [pltpu.make_async_copy(s, t, sems.at[i]) for i, (s, t) in enumerate(zip(sources, targets))]
    for copy in copies:
        copy.start()
    return copies


def select_kernel(
    rows_hbm,
    features_hbm,
    labels_hbm,
    counts_hbm,
    out_ref,
    rows_ref,
    features_ref,
    labels_ref,
    counts_ref,
    sems,
    *,
    digits,
):
    slots, stored = labels_ref.shape
    batches, group = rows_ref.shape
    width = features_ref.shape[1]
    part = stored // PARTS
    bands = [pl.ds(i * part, part) for i in range(PARTS)]
    copies = fetch(
        (rows_hbm, labels_hbm, counts_hbm, *[features_hbm.at[band] for band in bands]),
        (rows_ref, labels_ref, counts_ref, *[features_ref.at[band] for band in bands]),
        sems,
    )
    copies[0].wait()
    rows = batches * group
    one_hot = jnp.concatenate(
        [
            jnp.transpose(
                jnp.where(
                    lax.broadcasted_iota(jnp.int32, (stored, group), 0) == rows_ref[t : t + 1, :], 1.0, 0.0
                )
            )
            for t in range(batches)
        ],
        axis=0,
    ).astype(jnp.bfloat16)
    for copy in copies[1:]:
        copy.wait()
    ids = labels_ref[...]
    used = lax.broadcasted_iota(jnp.int32, (slots, stored), 0) < counts_ref[...]
    table = [(ids >> (8 * i)) & 255 for i in range(digits - 1)]
    table.append(jnp.where(used, ids >> (8 * (digits - 1)), NO_LABEL))
    table = jnp.concatenate(table, axis=0).astype(jnp.float32).astype(jnp.bfloat16)
    codes = across(table, one_hot)
    codes = [codes[i * slots : (i + 1) * slots, :] for i in range(digits)]
    codes += [jnp.zeros((slots, rows), jnp.float32)] * (digits % 2)
    start = rows * (width // LANES)
    for i in range(0, digits, 2):
        out_ref[start : start + slots, :] = jnp.concatenate(codes[i : i + 2], axis=1).astype(jnp.bfloat16)
        start += slots
    chosen = jnp.dot(one_hot, features_ref[...], preferred_element_type=jnp.float32).astype(jnp.bfloat16)
    for j in range(width // LANES):
        out_ref[j * rows : (j + 1) * rows, :] = chosen[:, j * LANES : (j + 1) * LANES]


def prepare_kernel(weights_hbm, momentum_hbm, after_ref, weights_ref, decayed_ref, low_ref, sems):
    copies = fetch((weights_hbm, momentum_hbm), (weights_ref, decayed_ref), sems)
    copies[0].wait()
    low_ref[...] = weights_ref[...].astype(jnp.bfloat16)
    copies[1].wait()
    decayed_ref[...] = decay_rate * decayed_ref[...]


def features_of(piece_refs, batch, batches, group, width):
    rows = batches * group
    starts = [j * rows + batch * group for j in range(width // LANES)]
    return jnp.concatenate(
        [jnp.concatenate([r[i : i + group, :] for r in piece_refs], axis=0) for i in starts], axis=1
    )


def ids_of(piece_refs, batches, group, width, slots, digits):
    rows = batches * group
    start = rows * (width // LANES)
    ids = []
    for r in piece_refs:
        total = 0.0
        for i in range(digits):
            at = start + slots * (i // 2)
            total = total + 256.0**i * r[at : at + slots, :].astype(jnp.float32)[:, rows * (i % 2) : rows * (i % 2 + 1)]
        ids.append(total)
    return [jnp.concatenate([t[:, b * group : (b + 1) * group] for t in ids], axis=1) for b in range(batches)]


def targets_of(ids, labels, base):
    slots, rows = ids.shape
    local = jnp.clip(ids - base, -1.0, float(labels)).astype(jnp.int32).astype(jnp.int16)
    label = lax.broadcasted_iota(jnp.int32, (labels, rows), 0).astype(jnp.int16)
    one, targets = jnp.ones((labels, rows), jnp.bfloat16), jnp.zeros((labels, rows), jnp.bfloat16)
    for k in range(slots):
        same = label == jnp.broadcast_to(local[k : k + 1, :], (labels, rows))
        targets = jnp.where(same, one, targets)
    return targets


def across(a, b):
    return lax.dot_general(a, b, (((1,), (1,)), ((), ())), preferred_element_type=jnp.float32)


def errors_of(logits, targets):
    return (1.0 / (1.0 + jnp.exp(-logits)) - targets.astype(jnp.float32)).astype(jnp.bfloat16)


def grads_of(errors, features):
    return jnp.dot(errors, features, preferred_element_type=jnp.float32)


def parts_kernel(base_ref, *refs, pieces, batches, group, slots, digits):
    piece_refs = refs[:pieces]
    weights_ref, decayed_ref, low_ref = refs[pieces : pieces + 3]
    *part_refs, first_ref, second_ref, targets_ref = refs[pieces + 3 :]
    share = pieces // len(part_refs)
    labels, width = weights_ref.shape
    half = labels // 2
    base = base_ref[0].astype(jnp.float32)
    chunks = [slice(c, min(c + COLUMNS, width)) for c in range(0, width, COLUMNS)]

    def put(t, errors, low_weights):
        for c, low in zip(chunks, low_weights):
            summed = lax.dot_general(
                errors, low, (((0,), (0,)), ((), ())), preferred_element_type=jnp.float32
            )
            for p in range(pieces):
                start = (2 * (p % share) + t) * group
                part_refs[p // share][start : start + group, c] = summed[p * group : (p + 1) * group, :]

    ids = ids_of(piece_refs, batches, group, width, slots, digits)
    features = features_of(piece_refs, 0, batches, group, width)
    logits = [across(low_ref[i * half : (i + 1) * half, :], features) for i in range(2)]
    targets = targets_of(ids[0], labels, base)
    errors = errors_of(jnp.concatenate(logits, axis=0), targets)
    first_ref[...] = errors
    next_features = features_of(piece_refs, 1, batches, group, width)
    targets_ref[...] = targets_of(ids[1], labels, base)
    next_low, logits = [], 0.0
    for c in chunks:
        momentum = decayed_ref[:, c] + grads_of(errors, features[:, c])
        low = (weights_ref[:, c] - learn_rate * momentum).astype(jnp.bfloat16)
        next_low.append(low)
        logits = logits + across(low, next_features[:, c])
    put(0, errors, [low_ref[:, c] for c in chunks])
    errors = errors_of(logits, targets_ref[...])
    second_ref[...] = errors
    put(1, errors, next_low)


def update_kernel(errors_ref, *refs, batch, batches, group):
    piece_refs = refs[:-4]
    weights_ref, momentum_ref, weights_out, momentum_out = refs[-4:]
    features = features_of(piece_refs, batch, batches, group, weights_ref.shape[1])
    momentum = momentum_ref[...] if batch == 0 else decay_rate * momentum_ref[...]
    momentum = momentum + grads_of(errors_ref[...], features)
    momentum_out[...] = momentum
    weights_out[...] = weights_ref[...] - learn_rate * momentum


def encode(blocks, out_ref):
    rows = TILE_ROWS * len(blocks)
    lane = lax.broadcasted_iota(jnp.int32, (TILE_ROWS, LANES), 1)
    tile = jnp.zeros((TILE_ROWS, LANES), jnp.float32)
    for g, values in enumerate(blocks):
        top = jnp.maximum(jnp.max(jnp.abs(values), axis=1, keepdims=True), SMALLEST)
        power = jnp.ceil(jnp.log(top * (1.0 / CODE_TOP)) * (1.0 / math.log(2.0)))
        codes = jnp.round(values * jnp.exp2(-power)).astype(jnp.int32).astype(jnp.int16)
        for j in range(values.shape[1] // LANES):
            start = j * rows + g * TILE_ROWS
            out_ref[start : start + TILE_ROWS, :] = codes[:, j * LANES : (j + 1) * LANES]
        tile = jnp.where(lane == g, power, tile)
    out_ref[out_ref.shape[0] - TILE_ROWS :, :] = tile.astype(jnp.int32).astype(jnp.int16)


def decode(codes_ref, g, rows, width):
    scale = jnp.exp2(codes_ref[codes_ref.shape[0] - TILE_ROWS :, :].astype(jnp.float32)[:, g : g + 1])
    start = g * TILE_ROWS
    return jnp.concatenate(
        [
            codes_ref[j * rows + start : j * rows + start + TILE_ROWS, :].astype(jnp.float32) * scale
            for j in range(width // LANES)
        ],
        axis=1,
    )


def coded_shape(rows, width):
    return jax.ShapeDtypeStruct((rows * (width // LANES) + TILE_ROWS, LANES), jnp.int16)


def fold_kernel(kept_ref, received_ref, *out_refs, coded):
    rows, width = kept_ref.shape
    blocks = []
    for g in range(rows // TILE_ROWS):
        at = slice(g * TILE_ROWS, (g + 1) * TILE_ROWS)
        total = kept_ref[at, :] + (decode(received_ref, g, rows, width) if coded else received_ref[at, :])
        if len(out_refs) == 2 and at.stop <= rows // 2:
            out_refs[0][at, :] = total
        else:
            blocks.append(total)
    encode(blocks, out_refs[-1])


def merged(refs, g, rows, width):
    own, *came = [decode(r, g, rows, width) for r in refs]
    total = own + came[-1]
    if len(came) == 3:
        total = total + (came[1] + came[0])
    return total


def merge_kernel(*refs, rows, width):
    encode([merged(refs[:-1], g, rows, width) for g in range(rows // TILE_ROWS)], refs[-1])


def last_merge_kernel(*refs, rows, width):
    *came, out_hbm, out_ref, sems = refs
    copies = []
    for g in range(rows // TILE_ROWS):
        at = pl.ds(g * TILE_ROWS, TILE_ROWS)
        out_ref[at, :] = merged(came, g, rows, width)
        copies.append(pltpu.make_async_copy(out_ref.at[at], out_hbm.at[at], sems.at[g]))
        copies[-1].start()
    for copy in copies:
        copy.wait()


def swap(x, axis, mask):
    size = lax.axis_size(axis)
    return lax.ppermute(x, axis, [(i, i ^ mask) for i in range(size)])


def masks_of(axis):
    size = lax.axis_size(axis)
    return [1 << b for b in range(size.bit_length() - 1)]


def per_device(pool_features, pool_labels, pool_counts, batch_rows, weights, momentum):
    labels, width = weights.shape
    stored, slots = pool_labels.shape
    batches, group = batch_rows.shape
    pieces = lax.axis_size("rows")
    batch_size = pieces * group
    digits = 2 if pieces * lax.axis_size("labels") * labels <= NO_LABEL * 256 else 3
    device_index = lax.axis_index("rows") * lax.axis_size("labels") + lax.axis_index("labels")
    base = (device_index * labels).astype(jnp.int32).reshape(1)
    vmem = pl.BlockSpec(memory_space=pltpu.VMEM)
    hbm = pl.BlockSpec(memory_space=pltpu.HBM)
    params = pltpu.CompilerParams(vmem_limit_bytes=VMEM_LIMIT)

    own = pl.pallas_call(
        functools.partial(select_kernel, digits=digits),
        out_shape=jax.ShapeDtypeStruct(
            (batches * group * (width // LANES) + slots * ((digits + 1) // 2), LANES), jnp.bfloat16
        ),
        in_specs=[hbm] * 4,
        out_specs=vmem,
        scratch_shapes=[
            pltpu.VMEM(batch_rows.shape, jnp.int32),
            pltpu.VMEM(pool_features.shape, jnp.bfloat16),
            pltpu.VMEM((slots, stored), jnp.int32),
            pltpu.VMEM((1, stored), jnp.int32),
            pltpu.SemaphoreType.DMA((3 + PARTS,)),
        ],
        compiler_params=params,
        name="select_rows",
    )(*[pltpu.with_memory_space_constraint(a, pltpu.HBM) for a in (batch_rows, pool_features, pool_labels.T, pool_counts.reshape(1, stored))])

    weights, momentum, low_weights = pl.pallas_call(
        prepare_kernel,
        out_shape=(
            jax.ShapeDtypeStruct(weights.shape, jnp.float32),
            jax.ShapeDtypeStruct(momentum.shape, jnp.float32),
            jax.ShapeDtypeStruct(weights.shape, jnp.bfloat16),
        ),
        in_specs=[hbm, hbm, vmem],
        out_specs=(vmem,) * 3,
        scratch_shapes=[pltpu.SemaphoreType.DMA((2,))],
        compiler_params=params,
        cost_estimate=pl.CostEstimate(
            flops=0, transcendentals=0, bytes_accessed=18 * labels * width
        ),
        name="prepare",
    )(*[pltpu.with_memory_space_constraint(a, pltpu.HBM) for a in (weights, momentum)], own)

    gathered = [own]
    for mask in reversed(masks_of("rows")):
        came = [swap(g, "rows", mask) for g in gathered]
        if mask > 1:
            *came, low_weights = lax.optimization_barrier((*came, low_weights))
        gathered = gathered + came

    quarter = batches * batch_size // 4
    kept, moved, kept_theirs, moved_theirs, first, second = pl.pallas_call(
        functools.partial(
            parts_kernel, pieces=pieces, batches=batches, group=group, slots=slots, digits=digits
        ),
        out_shape=(
            *[jax.ShapeDtypeStruct((quarter, width), jnp.float32)] * 4,
            jax.ShapeDtypeStruct((labels, batch_size), jnp.bfloat16),
            jax.ShapeDtypeStruct((labels, batch_size), jnp.bfloat16),
        ),
        in_specs=[pl.BlockSpec(memory_space=pltpu.SMEM)] + [vmem] * (pieces + 3),
        out_specs=(vmem,) * 6,
        scratch_shapes=[pltpu.VMEM((labels, batch_size), jnp.bfloat16)],
        compiler_params=params,
        name="parts",
    )(base, *gathered, weights, momentum, low_weights)

    def update(weights, momentum):
        for batch, errors in enumerate((first, second)):
            weights, momentum = pl.pallas_call(
                functools.partial(update_kernel, batch=batch, batches=batches, group=group),
                out_shape=(
                    jax.ShapeDtypeStruct(weights.shape, jnp.float32),
                    jax.ShapeDtypeStruct(momentum.shape, jnp.float32),
                ),
                in_specs=[vmem] * (pieces + 3),
                out_specs=(vmem,) * 2,
                compiler_params=params,
                cost_estimate=pl.CostEstimate(
                    flops=2 * batch_size * labels * width, transcendentals=0, bytes_accessed=16 * labels * width
                ),
                name=f"update_{batch}",
            )(errors, *gathered, weights, momentum)
        return weights, momentum

    def add(a, b, halve):
        rows = a.shape[0] // 2 if halve else a.shape[0]
        out = coded_shape(rows, width)
        return pl.pallas_call(
            functools.partial(fold_kernel, coded=b.dtype == jnp.int16),
            out_shape=(jax.ShapeDtypeStruct((rows, width), jnp.float32), out) if halve else out,
            in_specs=[vmem] * 2,
            out_specs=(vmem,) * 2 if halve else vmem,
            compiler_params=params,
            name="fold",
        )(a, b)

    masks = masks_of("rows")[1:]
    codes = add(moved, swap(moved_theirs, "rows", 1), False)
    received = swap(codes, "rows", masks[0])
    kept = kept + swap(kept_theirs, "rows", 1)
    received, kept, weights, momentum = lax.optimization_barrier((received, kept, *update(weights, momentum)))
    for mask in masks[1:]:
        kept, codes = add(kept, received, True)
        received = swap(codes, "rows", mask)
    rows = kept.shape[0]
    codes = add(kept, received, False)
    masks = masks_of("labels")
    steps = [masks[i : i + 2] for i in range(0, len(masks), 2)]
    for step in steps:
        partners = [step[0]] if len(step) == 1 else [step[0], step[1], step[0] | step[1]]
        came = [swap(codes, "labels", mask) for mask in reversed(partners)]
        if step is not steps[-1]:
            codes = pl.pallas_call(
                functools.partial(merge_kernel, rows=rows, width=width),
                out_shape=coded_shape(rows, width),
                in_specs=[vmem] * (1 + len(came)),
                out_specs=vmem,
                compiler_params=params,
                name="merge",
            )(codes, *came)
    parts = pl.pallas_call(
        functools.partial(last_merge_kernel, rows=rows, width=width),
        out_shape=jax.ShapeDtypeStruct((rows, width), jnp.float32),
        in_specs=[vmem] * (1 + len(came)),
        out_specs=hbm,
        scratch_shapes=[
            pltpu.VMEM((rows, width), jnp.float32),
            pltpu.SemaphoreType.DMA((rows // TILE_ROWS,)),
        ],
        compiler_params=params,
        name="last_merge",
    )(codes, *came)
    return weights, momentum, parts.reshape(batches, group, width)


def solution(mesh):
    in_specs = (
        P("rows", None),
        P("rows", None),
        P("rows"),
        P(None, "rows"),
        P(("rows", "labels"), None),
        P(("rows", "labels"), None),
    )
    out_specs = (P(("rows", "labels"), None), P(("rows", "labels"), None), P(None, "rows", None))
    return jax.shard_map(
        per_device, mesh=mesh, in_specs=in_specs, out_specs=out_specs, check_vma=False
    )
```

```python
import functools
import math

import jax
import jax.numpy as jnp
from jax import lax
from jax.experimental import pallas as pl
from jax.experimental.pallas import tpu as pltpu
from jax.sharding import PartitionSpec as P

learn_rate = 0.001
decay_rate = 0.9
LANES = 128
NO_LABEL = 255
VMEM_LIMIT = 16 << 20
COLUMNS = 256
PARTS = 4
TILE_ROWS = 16
CODE_TOP = 32000.0
SMALLEST = 1e-30


def fetch(sources, targets, sems):
    copies = [pltpu.make_async_copy(s, t, sems.at[i]) for i, (s, t) in enumerate(zip(sources, targets))]
    for copy in copies:
        copy.start()
    return copies


def select_kernel(
    rows_hbm,
    features_hbm,
    labels_hbm,
    counts_hbm,
    out_ref,
    rows_ref,
    features_ref,
    labels_ref,
    counts_ref,
    sems,
    *,
    digits,
):
    slots, stored = labels_ref.shape
    batches, group = rows_ref.shape
    width = features_ref.shape[1]
    part = stored // PARTS
    bands = [pl.ds(i * part, part) for i in range(PARTS)]
    copies = fetch(
        (*[features_hbm.at[band] for band in bands], rows_hbm, labels_hbm, counts_hbm),
        (*[features_ref.at[band] for band in bands], rows_ref, labels_ref, counts_ref),
        sems,
    )
    copies[PARTS].wait()
    rows = batches * group
    one_hot = jnp.concatenate(
        [
            jnp.transpose(
                jnp.where(
                    lax.broadcasted_iota(jnp.int32, (stored, group), 0) == rows_ref[t : t + 1, :], 1.0, 0.0
                )
            )
            for t in range(batches)
        ],
        axis=0,
    ).astype(jnp.bfloat16)
    for copy in copies[:PARTS] + copies[PARTS + 1 :]:
        copy.wait()
    ids = labels_ref[...]
    used = lax.broadcasted_iota(jnp.int32, (slots, stored), 0) < counts_ref[...]
    table = [(ids >> (8 * i)) & 255 for i in range(digits - 1)]
    table.append(jnp.where(used, ids >> (8 * (digits - 1)), NO_LABEL))
    table = jnp.concatenate(table, axis=0).astype(jnp.float32).astype(jnp.bfloat16)
    codes = across(table, one_hot)
    codes = [codes[i * slots : (i + 1) * slots, :] for i in range(digits)]
    codes += [jnp.zeros((slots, rows), jnp.float32)] * (digits % 2)
    start = rows * (width // LANES)
    for i in range(0, digits, 2):
        out_ref[start : start + slots, :] = jnp.concatenate(codes[i : i + 2], axis=1).astype(jnp.bfloat16)
        start += slots
    chosen = jnp.dot(one_hot, features_ref[...], preferred_element_type=jnp.float32).astype(jnp.bfloat16)
    for j in range(width // LANES):
        out_ref[j * rows : (j + 1) * rows, :] = chosen[:, j * LANES : (j + 1) * LANES]


def prepare_kernel(weights_hbm, momentum_hbm, after_ref, weights_ref, decayed_ref, low_ref, sems):
    copies = fetch((weights_hbm, momentum_hbm), (weights_ref, decayed_ref), sems)
    copies[0].wait()
    low_ref[...] = weights_ref[...].astype(jnp.bfloat16)
    copies[1].wait()
    decayed_ref[...] = decay_rate * decayed_ref[...]


def features_of(piece_refs, batch, batches, group, width):
    rows = batches * group
    starts = [j * rows + batch * group for j in range(width // LANES)]
    return jnp.concatenate(
        [jnp.concatenate([r[i : i + group, :] for r in piece_refs], axis=0) for i in starts], axis=1
    )


def ids_of(piece_refs, batches, group, width, slots, digits):
    rows = batches * group
    start = rows * (width // LANES)
    ids = []
    for r in piece_refs:
        total = 0.0
        for i in range(digits):
            at = start + slots * (i // 2)
            total = total + 256.0**i * r[at : at + slots, :].astype(jnp.float32)[:, rows * (i % 2) : rows * (i % 2 + 1)]
        ids.append(total)
    return [jnp.concatenate([t[:, b * group : (b + 1) * group] for t in ids], axis=1) for b in range(batches)]


def targets_of(ids, labels, base):
    slots, rows = ids.shape
    local = jnp.clip(ids - base, -1.0, float(labels)).astype(jnp.int32).astype(jnp.int16)
    label = lax.broadcasted_iota(jnp.int32, (labels, rows), 0).astype(jnp.int16)
    one, targets = jnp.ones((labels, rows), jnp.bfloat16), jnp.zeros((labels, rows), jnp.bfloat16)
    for k in range(slots):
        same = label == jnp.broadcast_to(local[k : k + 1, :], (labels, rows))
        targets = jnp.where(same, one, targets)
    return targets


def across(a, b):
    return lax.dot_general(a, b, (((1,), (1,)), ((), ())), preferred_element_type=jnp.float32)


def errors_of(logits, targets):
    return (1.0 / (1.0 + jnp.exp(-logits)) - targets.astype(jnp.float32)).astype(jnp.bfloat16)


def grads_of(errors, features):
    return jnp.dot(errors, features, preferred_element_type=jnp.float32)


def parts_kernel(base_ref, *refs, pieces, batches, group, slots, digits):
    piece_refs = refs[:pieces]
    weights_ref, decayed_ref, low_ref = refs[pieces : pieces + 3]
    *part_refs, first_ref, second_ref, targets_ref = refs[pieces + 3 :]
    share = pieces // len(part_refs)
    labels, width = weights_ref.shape
    half = labels // 2
    base = base_ref[0].astype(jnp.float32)
    chunks = [slice(c, min(c + COLUMNS, width)) for c in range(0, width, COLUMNS)]

    def put(t, errors, low_weights):
        for c, low in zip(chunks, low_weights):
            summed = lax.dot_general(
                errors, low, (((0,), (0,)), ((), ())), preferred_element_type=jnp.float32
            )
            for p in range(pieces):
                start = (2 * (p % share) + t) * group
                part_refs[p // share][start : start + group, c] = summed[p * group : (p + 1) * group, :]

    ids = ids_of(piece_refs, batches, group, width, slots, digits)
    features = features_of(piece_refs, 0, batches, group, width)
    logits = [across(low_ref[i * half : (i + 1) * half, :], features) for i in range(2)]
    targets = targets_of(ids[0], labels, base)
    errors = errors_of(jnp.concatenate(logits, axis=0), targets)
    first_ref[...] = errors
    next_features = features_of(piece_refs, 1, batches, group, width)
    targets_ref[...] = targets_of(ids[1], labels, base)
    next_low, logits = [], 0.0
    for c in chunks:
        momentum = decayed_ref[:, c] + grads_of(errors, features[:, c])
        low = (weights_ref[:, c] - learn_rate * momentum).astype(jnp.bfloat16)
        next_low.append(low)
        logits = logits + across(low, next_features[:, c])
    put(0, errors, [low_ref[:, c] for c in chunks])
    errors = errors_of(logits, targets_ref[...])
    second_ref[...] = errors
    put(1, errors, next_low)


def update_kernel(errors_ref, *refs, batch, batches, group):
    piece_refs = refs[:-4]
    weights_ref, momentum_ref, weights_out, momentum_out = refs[-4:]
    features = features_of(piece_refs, batch, batches, group, weights_ref.shape[1])
    momentum = momentum_ref[...] if batch == 0 else decay_rate * momentum_ref[...]
    momentum = momentum + grads_of(errors_ref[...], features)
    momentum_out[...] = momentum
    weights_out[...] = weights_ref[...] - learn_rate * momentum


def encode(blocks, out_ref):
    rows = TILE_ROWS * len(blocks)
    lane = lax.broadcasted_iota(jnp.int32, (TILE_ROWS, LANES), 1)
    tile = jnp.zeros((TILE_ROWS, LANES), jnp.float32)
    for g, values in enumerate(blocks):
        top = jnp.maximum(jnp.max(jnp.abs(values), axis=1, keepdims=True), SMALLEST)
        power = jnp.ceil(jnp.log(top * (1.0 / CODE_TOP)) * (1.0 / math.log(2.0)))
        codes = jnp.round(values * jnp.exp2(-power)).astype(jnp.int32).astype(jnp.int16)
        for j in range(values.shape[1] // LANES):
            start = j * rows + g * TILE_ROWS
            out_ref[start : start + TILE_ROWS, :] = codes[:, j * LANES : (j + 1) * LANES]
        tile = jnp.where(lane == g, power, tile)
    out_ref[out_ref.shape[0] - TILE_ROWS :, :] = tile.astype(jnp.int32).astype(jnp.int16)


def decode(codes_ref, g, rows, width):
    scale = jnp.exp2(codes_ref[codes_ref.shape[0] - TILE_ROWS :, :].astype(jnp.float32)[:, g : g + 1])
    start = g * TILE_ROWS
    return jnp.concatenate(
        [
            codes_ref[j * rows + start : j * rows + start + TILE_ROWS, :].astype(jnp.float32) * scale
            for j in range(width // LANES)
        ],
        axis=1,
    )


def coded_shape(rows, width):
    return jax.ShapeDtypeStruct((rows * (width // LANES) + TILE_ROWS, LANES), jnp.int16)


def fold_kernel(kept_ref, received_ref, *out_refs, coded):
    rows, width = kept_ref.shape
    blocks = []
    for g in range(rows // TILE_ROWS):
        at = slice(g * TILE_ROWS, (g + 1) * TILE_ROWS)
        total = kept_ref[at, :] + (decode(received_ref, g, rows, width) if coded else received_ref[at, :])
        if len(out_refs) == 2 and at.stop <= rows // 2:
            out_refs[0][at, :] = total
        else:
            blocks.append(total)
    encode(blocks, out_refs[-1])


def merged(refs, g, rows, width):
    own, *came = [decode(r, g, rows, width) for r in refs]
    total = own + came[-1]
    if len(came) == 3:
        total = total + (came[1] + came[0])
    return total


def merge_kernel(*refs, rows, width):
    encode([merged(refs[:-1], g, rows, width) for g in range(rows // TILE_ROWS)], refs[-1])


def last_merge_kernel(*refs, rows, width):
    *came, out_hbm, out_ref, sems = refs
    copies = []
    for g in range(rows // TILE_ROWS):
        at = pl.ds(g * TILE_ROWS, TILE_ROWS)
        out_ref[at, :] = merged(came, g, rows, width)
        copies.append(pltpu.make_async_copy(out_ref.at[at], out_hbm.at[at], sems.at[g]))
        copies[-1].start()
    for copy in copies:
        copy.wait()


def swap(x, axis, mask):
    size = lax.axis_size(axis)
    return lax.ppermute(x, axis, [(i, i ^ mask) for i in range(size)])


def masks_of(axis):
    size = lax.axis_size(axis)
    return [1 << b for b in range(size.bit_length() - 1)]


def per_device(pool_features, pool_labels, pool_counts, batch_rows, weights, momentum):
    labels, width = weights.shape
    stored, slots = pool_labels.shape
    batches, group = batch_rows.shape
    pieces = lax.axis_size("rows")
    batch_size = pieces * group
    digits = 2 if pieces * lax.axis_size("labels") * labels <= NO_LABEL * 256 else 3
    device_index = lax.axis_index("rows") * lax.axis_size("labels") + lax.axis_index("labels")
    base = (device_index * labels).astype(jnp.int32).reshape(1)
    vmem = pl.BlockSpec(memory_space=pltpu.VMEM)
    hbm = pl.BlockSpec(memory_space=pltpu.HBM)
    params = pltpu.CompilerParams(vmem_limit_bytes=VMEM_LIMIT)

    own = pl.pallas_call(
        functools.partial(select_kernel, digits=digits),
        out_shape=jax.ShapeDtypeStruct(
            (batches * group * (width // LANES) + slots * ((digits + 1) // 2), LANES), jnp.bfloat16
        ),
        in_specs=[hbm] * 4,
        out_specs=vmem,
        scratch_shapes=[
            pltpu.VMEM(batch_rows.shape, jnp.int32),
            pltpu.VMEM(pool_features.shape, jnp.bfloat16),
            pltpu.VMEM((slots, stored), jnp.int32),
            pltpu.VMEM((1, stored), jnp.int32),
            pltpu.SemaphoreType.DMA((3 + PARTS,)),
        ],
        compiler_params=params,
        name="select_rows",
    )(*[pltpu.with_memory_space_constraint(a, pltpu.HBM) for a in (batch_rows, pool_features, pool_labels.T, pool_counts.reshape(1, stored))])

    weights, momentum, low_weights = pl.pallas_call(
        prepare_kernel,
        out_shape=(
            jax.ShapeDtypeStruct(weights.shape, jnp.float32),
            jax.ShapeDtypeStruct(momentum.shape, jnp.float32),
            jax.ShapeDtypeStruct(weights.shape, jnp.bfloat16),
        ),
        in_specs=[hbm, hbm, vmem],
        out_specs=(vmem,) * 3,
        scratch_shapes=[pltpu.SemaphoreType.DMA((2,))],
        compiler_params=params,
        cost_estimate=pl.CostEstimate(
            flops=0, transcendentals=0, bytes_accessed=18 * labels * width
        ),
        name="prepare",
    )(*[pltpu.with_memory_space_constraint(a, pltpu.HBM) for a in (weights, momentum)], own)

    gathered = [own]
    for mask in reversed(masks_of("rows")):
        came = [swap(g, "rows", mask) for g in gathered]
        if mask > 1:
            *came, low_weights = lax.optimization_barrier((*came, low_weights))
        gathered = gathered + came

    quarter = batches * batch_size // 4
    kept, moved, kept_theirs, moved_theirs, first, second = pl.pallas_call(
        functools.partial(
            parts_kernel, pieces=pieces, batches=batches, group=group, slots=slots, digits=digits
        ),
        out_shape=(
            *[jax.ShapeDtypeStruct((quarter, width), jnp.float32)] * 4,
            jax.ShapeDtypeStruct((labels, batch_size), jnp.bfloat16),
            jax.ShapeDtypeStruct((labels, batch_size), jnp.bfloat16),
        ),
        in_specs=[pl.BlockSpec(memory_space=pltpu.SMEM)] + [vmem] * (pieces + 3),
        out_specs=(vmem,) * 6,
        scratch_shapes=[pltpu.VMEM((labels, batch_size), jnp.bfloat16)],
        compiler_params=params,
        name="parts",
    )(base, *gathered, weights, momentum, low_weights)

    def update(weights, momentum):
        for batch, errors in enumerate((first, second)):
            weights, momentum = pl.pallas_call(
                functools.partial(update_kernel, batch=batch, batches=batches, group=group),
                out_shape=(
                    jax.ShapeDtypeStruct(weights.shape, jnp.float32),
                    jax.ShapeDtypeStruct(momentum.shape, jnp.float32),
                ),
                in_specs=[vmem] * (pieces + 3),
                out_specs=(vmem,) * 2,
                compiler_params=params,
                cost_estimate=pl.CostEstimate(
                    flops=2 * batch_size * labels * width, transcendentals=0, bytes_accessed=16 * labels * width
                ),
                name=f"update_{batch}",
            )(errors, *gathered, weights, momentum)
        return weights, momentum

    def add(a, b, halve):
        rows = a.shape[0] // 2 if halve else a.shape[0]
        out = coded_shape(rows, width)
        return pl.pallas_call(
            functools.partial(fold_kernel, coded=b.dtype == jnp.int16),
            out_shape=(jax.ShapeDtypeStruct((rows, width), jnp.float32), out) if halve else out,
            in_specs=[vmem] * 2,
            out_specs=(vmem,) * 2 if halve else vmem,
            compiler_params=params,
            name="fold",
        )(a, b)

    masks = masks_of("rows")[1:]
    codes = add(moved, swap(moved_theirs, "rows", 1), False)
    received = swap(codes, "rows", masks[0])
    kept = kept + swap(kept_theirs, "rows", 1)
    received, kept, weights, momentum = lax.optimization_barrier((received, kept, *update(weights, momentum)))
    for mask in masks[1:]:
        kept, codes = add(kept, received, True)
        received = swap(codes, "rows", mask)
    rows = kept.shape[0]
    codes = add(kept, received, False)
    masks = masks_of("labels")
    steps = [masks[i : i + 2] for i in range(0, len(masks), 2)]
    for step in steps:
        partners = [step[0]] if len(step) == 1 else [step[0], step[1], step[0] | step[1]]
        came = [swap(codes, "labels", mask) for mask in reversed(partners)]
        if step is not steps[-1]:
            codes = pl.pallas_call(
                functools.partial(merge_kernel, rows=rows, width=width),
                out_shape=coded_shape(rows, width),
                in_specs=[vmem] * (1 + len(came)),
                out_specs=vmem,
                compiler_params=params,
                name="merge",
            )(codes, *came)
    parts = pl.pallas_call(
        functools.partial(last_merge_kernel, rows=rows, width=width),
        out_shape=jax.ShapeDtypeStruct((rows, width), jnp.float32),
        in_specs=[vmem] * (1 + len(came)),
        out_specs=hbm,
        scratch_shapes=[
            pltpu.VMEM((rows, width), jnp.float32),
            pltpu.SemaphoreType.DMA((rows // TILE_ROWS,)),
        ],
        compiler_params=params,
        name="last_merge",
    )(codes, *came)
    return weights, momentum, parts.reshape(batches, group, width)


def solution(mesh):
    in_specs = (
        P("rows", None),
        P("rows", None),
        P("rows"),
        P(None, "rows"),
        P(("rows", "labels"), None),
        P(("rows", "labels"), None),
    )
    out_specs = (P(("rows", "labels"), None), P(("rows", "labels"), None), P(None, "rows", None))
    return jax.shard_map(
        per_device, mesh=mesh, in_specs=in_specs, out_specs=out_specs, check_vma=False
    )
```

```python
import functools
import math

import jax
import jax.numpy as jnp
from jax import lax
from jax.experimental import pallas as pl
from jax.experimental.pallas import tpu as pltpu
from jax.sharding import PartitionSpec as P

learn_rate = 0.001
decay_rate = 0.9
LANES = 128
NO_LABEL = 255
VMEM_LIMIT = 16 << 20
COLUMNS = 256
PARTS = 4
TILE_ROWS = 16
CODE_TOP = 32000.0
SMALLEST = 1e-30


def fetch(sources, targets, sems):
    copies = [pltpu.make_async_copy(s, t, sems.at[i]) for i, (s, t) in enumerate(zip(sources, targets))]
    for copy in copies:
        copy.start()
    return copies


def select_kernel(
    rows_hbm,
    features_hbm,
    labels_hbm,
    counts_hbm,
    out_ref,
    rows_ref,
    features_ref,
    labels_ref,
    counts_ref,
    sems,
    *,
    digits,
):
    slots, stored = labels_ref.shape
    batches, group = rows_ref.shape
    width = features_ref.shape[1]
    part = stored // PARTS
    bands = [pl.ds(i * part, part) for i in range(PARTS)]
    copies = fetch(
        (*[features_hbm.at[band] for band in bands], rows_hbm, labels_hbm, counts_hbm),
        (*[features_ref.at[band] for band in bands], rows_ref, labels_ref, counts_ref),
        sems,
    )
    copies[PARTS].wait()
    rows = batches * group
    one_hot = jnp.concatenate(
        [
            jnp.transpose(
                jnp.where(
                    lax.broadcasted_iota(jnp.int32, (stored, group), 0) == rows_ref[t : t + 1, :], 1.0, 0.0
                )
            )
            for t in range(batches)
        ],
        axis=0,
    ).astype(jnp.bfloat16)
    for copy in copies[:PARTS] + copies[PARTS + 1 :]:
        copy.wait()
    ids = labels_ref[...]
    used = lax.broadcasted_iota(jnp.int32, (slots, stored), 0) < counts_ref[...]
    table = [(ids >> (8 * i)) & 255 for i in range(digits - 1)]
    table.append(jnp.where(used, ids >> (8 * (digits - 1)), NO_LABEL))
    table = jnp.concatenate(table, axis=0).astype(jnp.float32).astype(jnp.bfloat16)
    codes = across(table, one_hot)
    codes = [codes[i * slots : (i + 1) * slots, :] for i in range(digits)]
    codes += [jnp.zeros((slots, rows), jnp.float32)] * (digits % 2)
    start = rows * (width // LANES)
    for i in range(0, digits, 2):
        out_ref[start : start + slots, :] = jnp.concatenate(codes[i : i + 2], axis=1).astype(jnp.bfloat16)
        start += slots
    chosen = jnp.dot(one_hot, features_ref[...], preferred_element_type=jnp.float32).astype(jnp.bfloat16)
    for j in range(width // LANES):
        out_ref[j * rows : (j + 1) * rows, :] = chosen[:, j * LANES : (j + 1) * LANES]


def prepare_kernel(weights_hbm, momentum_hbm, after_ref, weights_ref, decayed_ref, low_ref, sems):
    copies = fetch((weights_hbm, momentum_hbm), (weights_ref, decayed_ref), sems)
    copies[0].wait()
    low_ref[...] = weights_ref[...].astype(jnp.bfloat16)
    copies[1].wait()
    decayed_ref[...] = decay_rate * decayed_ref[...]


def features_of(piece_refs, batch, batches, group, width):
    rows = batches * group
    starts = [j * rows + batch * group for j in range(width // LANES)]
    return jnp.concatenate(
        [jnp.concatenate([r[i : i + group, :] for r in piece_refs], axis=0) for i in starts], axis=1
    )


def ids_of(piece_refs, batches, group, width, slots, digits):
    rows = batches * group
    start = rows * (width // LANES)
    ids = []
    for r in piece_refs:
        total = 0.0
        for i in range(digits):
            at = start + slots * (i // 2)
            total = total + 256.0**i * r[at : at + slots, :].astype(jnp.float32)[:, rows * (i % 2) : rows * (i % 2 + 1)]
        ids.append(total)
    return [jnp.concatenate([t[:, b * group : (b + 1) * group] for t in ids], axis=1) for b in range(batches)]


def targets_of(ids, labels, base):
    slots, rows = ids.shape
    local = jnp.clip(ids - base, -1.0, float(labels)).astype(jnp.int32).astype(jnp.int16)
    label = lax.broadcasted_iota(jnp.int32, (labels, rows), 0).astype(jnp.int16)
    one, targets = jnp.ones((labels, rows), jnp.bfloat16), jnp.zeros((labels, rows), jnp.bfloat16)
    for k in range(slots):
        same = label == jnp.broadcast_to(local[k : k + 1, :], (labels, rows))
        targets = jnp.where(same, one, targets)
    return targets


def across(a, b):
    return lax.dot_general(a, b, (((1,), (1,)), ((), ())), preferred_element_type=jnp.float32)


def errors_of(logits, targets):
    return (1.0 / (1.0 + jnp.exp(-logits)) - targets.astype(jnp.float32)).astype(jnp.bfloat16)


def grads_of(errors, features):
    return jnp.dot(errors, features, preferred_element_type=jnp.float32)


def parts_kernel(base_ref, *refs, pieces, batches, group, slots, digits):
    piece_refs = refs[:pieces]
    weights_ref, decayed_ref, low_ref = refs[pieces : pieces + 3]
    *part_refs, first_ref, second_ref, targets_ref = refs[pieces + 3 :]
    share = pieces // len(part_refs)
    labels, width = weights_ref.shape
    half = labels // 2
    base = base_ref[0].astype(jnp.float32)
    chunks = [slice(c, min(c + COLUMNS, width)) for c in range(0, width, COLUMNS)]

    def put(t, errors, low_weights):
        for c, low in zip(chunks, low_weights):
            summed = lax.dot_general(
                errors, low, (((0,), (0,)), ((), ())), preferred_element_type=jnp.float32
            )
            for p in range(pieces):
                start = (2 * (p % share) + t) * group
                part_refs[p // share][start : start + group, c] = summed[p * group : (p + 1) * group, :]

    ids = ids_of(piece_refs, batches, group, width, slots, digits)
    features = features_of(piece_refs, 0, batches, group, width)
    logits = [across(low_ref[i * half : (i + 1) * half, :], features) for i in range(2)]
    targets = targets_of(ids[0], labels, base)
    errors = errors_of(jnp.concatenate(logits, axis=0), targets)
    first_ref[...] = errors
    next_features = features_of(piece_refs, 1, batches, group, width)
    targets_ref[...] = targets_of(ids[1], labels, base)
    next_low = []
    for c in chunks:
        momentum = decayed_ref[:, c] + grads_of(errors, features[:, c])
        low = (weights_ref[:, c] - learn_rate * momentum).astype(jnp.bfloat16)
        next_low.append(low)
    whole = jnp.concatenate(next_low, axis=1)
    logits = jnp.concatenate([across(whole[i * half : (i + 1) * half, :], next_features) for i in range(2)], axis=0)
    put(0, errors, [low_ref[:, c] for c in chunks])
    errors = errors_of(logits, targets_ref[...])
    second_ref[...] = errors
    put(1, errors, next_low)


def update_kernel(errors_ref, *refs, batch, batches, group):
    piece_refs = refs[:-4]
    weights_ref, momentum_ref, weights_out, momentum_out = refs[-4:]
    features = features_of(piece_refs, batch, batches, group, weights_ref.shape[1])
    momentum = momentum_ref[...] if batch == 0 else decay_rate * momentum_ref[...]
    momentum = momentum + grads_of(errors_ref[...], features)
    momentum_out[...] = momentum
    weights_out[...] = weights_ref[...] - learn_rate * momentum


def encode(blocks, out_ref):
    rows = TILE_ROWS * len(blocks)
    lane = lax.broadcasted_iota(jnp.int32, (TILE_ROWS, LANES), 1)
    tile = jnp.zeros((TILE_ROWS, LANES), jnp.float32)
    for g, values in enumerate(blocks):
        top = jnp.maximum(jnp.max(jnp.abs(values), axis=1, keepdims=True), SMALLEST)
        power = jnp.ceil(jnp.log(top * (1.0 / CODE_TOP)) * (1.0 / math.log(2.0)))
        codes = jnp.round(values * jnp.exp2(-power)).astype(jnp.int32).astype(jnp.int16)
        for j in range(values.shape[1] // LANES):
            start = j * rows + g * TILE_ROWS
            out_ref[start : start + TILE_ROWS, :] = codes[:, j * LANES : (j + 1) * LANES]
        tile = jnp.where(lane == g, power, tile)
    out_ref[out_ref.shape[0] - TILE_ROWS :, :] = tile.astype(jnp.int32).astype(jnp.int16)


def decode(codes_ref, g, rows, width):
    scale = jnp.exp2(codes_ref[codes_ref.shape[0] - TILE_ROWS :, :].astype(jnp.float32)[:, g : g + 1])
    start = g * TILE_ROWS
    return jnp.concatenate(
        [
            codes_ref[j * rows + start : j * rows + start + TILE_ROWS, :].astype(jnp.float32) * scale
            for j in range(width // LANES)
        ],
        axis=1,
    )


def coded_shape(rows, width):
    return jax.ShapeDtypeStruct((rows * (width // LANES) + TILE_ROWS, LANES), jnp.int16)


def fold_kernel(kept_ref, received_ref, *out_refs, coded):
    rows, width = kept_ref.shape
    blocks = []
    for g in range(rows // TILE_ROWS):
        at = slice(g * TILE_ROWS, (g + 1) * TILE_ROWS)
        total = kept_ref[at, :] + (decode(received_ref, g, rows, width) if coded else received_ref[at, :])
        if len(out_refs) == 2 and at.stop <= rows // 2:
            out_refs[0][at, :] = total
        else:
            blocks.append(total)
    encode(blocks, out_refs[-1])


def merged(refs, g, rows, width):
    own, *came = [decode(r, g, rows, width) for r in refs]
    total = own + came[-1]
    if len(came) == 3:
        total = total + (came[1] + came[0])
    return total


def merge_kernel(*refs, rows, width):
    encode([merged(refs[:-1], g, rows, width) for g in range(rows // TILE_ROWS)], refs[-1])


def last_merge_kernel(*refs, rows, width):
    *came, out_hbm, out_ref, sems = refs
    copies = []
    for g in range(rows // TILE_ROWS):
        at = pl.ds(g * TILE_ROWS, TILE_ROWS)
        out_ref[at, :] = merged(came, g, rows, width)
        copies.append(pltpu.make_async_copy(out_ref.at[at], out_hbm.at[at], sems.at[g]))
        copies[-1].start()
    for copy in copies:
        copy.wait()


def swap(x, axis, mask):
    size = lax.axis_size(axis)
    return lax.ppermute(x, axis, [(i, i ^ mask) for i in range(size)])


def masks_of(axis):
    size = lax.axis_size(axis)
    return [1 << b for b in range(size.bit_length() - 1)]


def per_device(pool_features, pool_labels, pool_counts, batch_rows, weights, momentum):
    labels, width = weights.shape
    stored, slots = pool_labels.shape
    batches, group = batch_rows.shape
    pieces = lax.axis_size("rows")
    batch_size = pieces * group
    digits = 2 if pieces * lax.axis_size("labels") * labels <= NO_LABEL * 256 else 3
    device_index = lax.axis_index("rows") * lax.axis_size("labels") + lax.axis_index("labels")
    base = (device_index * labels).astype(jnp.int32).reshape(1)
    vmem = pl.BlockSpec(memory_space=pltpu.VMEM)
    hbm = pl.BlockSpec(memory_space=pltpu.HBM)
    params = pltpu.CompilerParams(vmem_limit_bytes=VMEM_LIMIT)

    own = pl.pallas_call(
        functools.partial(select_kernel, digits=digits),
        out_shape=jax.ShapeDtypeStruct(
            (batches * group * (width // LANES) + slots * ((digits + 1) // 2), LANES), jnp.bfloat16
        ),
        in_specs=[hbm] * 4,
        out_specs=vmem,
        scratch_shapes=[
            pltpu.VMEM(batch_rows.shape, jnp.int32),
            pltpu.VMEM(pool_features.shape, jnp.bfloat16),
            pltpu.VMEM((slots, stored), jnp.int32),
            pltpu.VMEM((1, stored), jnp.int32),
            pltpu.SemaphoreType.DMA((3 + PARTS,)),
        ],
        compiler_params=params,
        name="select_rows",
    )(*[pltpu.with_memory_space_constraint(a, pltpu.HBM) for a in (batch_rows, pool_features, pool_labels.T, pool_counts.reshape(1, stored))])

    weights, momentum, low_weights = pl.pallas_call(
        prepare_kernel,
        out_shape=(
            jax.ShapeDtypeStruct(weights.shape, jnp.float32),
            jax.ShapeDtypeStruct(momentum.shape, jnp.float32),
            jax.ShapeDtypeStruct(weights.shape, jnp.bfloat16),
        ),
        in_specs=[hbm, hbm, vmem],
        out_specs=(vmem,) * 3,
        scratch_shapes=[pltpu.SemaphoreType.DMA((2,))],
        compiler_params=params,
        cost_estimate=pl.CostEstimate(
            flops=0, transcendentals=0, bytes_accessed=18 * labels * width
        ),
        name="prepare",
    )(*[pltpu.with_memory_space_constraint(a, pltpu.HBM) for a in (weights, momentum)], own)

    gathered = [own]
    for mask in reversed(masks_of("rows")):
        came = [swap(g, "rows", mask) for g in gathered]
        if mask > 1:
            *came, low_weights = lax.optimization_barrier((*came, low_weights))
        gathered = gathered + came

    quarter = batches * batch_size // 4
    kept, moved, kept_theirs, moved_theirs, first, second = pl.pallas_call(
        functools.partial(
            parts_kernel, pieces=pieces, batches=batches, group=group, slots=slots, digits=digits
        ),
        out_shape=(
            *[jax.ShapeDtypeStruct((quarter, width), jnp.float32)] * 4,
            jax.ShapeDtypeStruct((labels, batch_size), jnp.bfloat16),
            jax.ShapeDtypeStruct((labels, batch_size), jnp.bfloat16),
        ),
        in_specs=[pl.BlockSpec(memory_space=pltpu.SMEM)] + [vmem] * (pieces + 3),
        out_specs=(vmem,) * 6,
        scratch_shapes=[pltpu.VMEM((labels, batch_size), jnp.bfloat16)],
        compiler_params=params,
        name="parts",
    )(base, *gathered, weights, momentum, low_weights)

    def update(weights, momentum):
        for batch, errors in enumerate((first, second)):
            weights, momentum = pl.pallas_call(
                functools.partial(update_kernel, batch=batch, batches=batches, group=group),
                out_shape=(
                    jax.ShapeDtypeStruct(weights.shape, jnp.float32),
                    jax.ShapeDtypeStruct(momentum.shape, jnp.float32),
                ),
                in_specs=[vmem] * (pieces + 3),
                out_specs=(vmem,) * 2,
                compiler_params=params,
                cost_estimate=pl.CostEstimate(
                    flops=2 * batch_size * labels * width, transcendentals=0, bytes_accessed=16 * labels * width
                ),
                name=f"update_{batch}",
            )(errors, *gathered, weights, momentum)
        return weights, momentum

    def add(a, b, halve):
        rows = a.shape[0] // 2 if halve else a.shape[0]
        out = coded_shape(rows, width)
        return pl.pallas_call(
            functools.partial(fold_kernel, coded=b.dtype == jnp.int16),
            out_shape=(jax.ShapeDtypeStruct((rows, width), jnp.float32), out) if halve else out,
            in_specs=[vmem] * 2,
            out_specs=(vmem,) * 2 if halve else vmem,
            compiler_params=params,
            name="fold",
        )(a, b)

    masks = masks_of("rows")[1:]
    codes = add(moved, swap(moved_theirs, "rows", 1), False)
    received = swap(codes, "rows", masks[0])
    kept = kept + swap(kept_theirs, "rows", 1)
    received, kept, weights, momentum = lax.optimization_barrier((received, kept, *update(weights, momentum)))
    for mask in masks[1:]:
        kept, codes = add(kept, received, True)
        received = swap(codes, "rows", mask)
    rows = kept.shape[0]
    codes = add(kept, received, False)
    masks = masks_of("labels")
    steps = [masks[i : i + 2] for i in range(0, len(masks), 2)]
    for step in steps:
        partners = [step[0]] if len(step) == 1 else [step[0], step[1], step[0] | step[1]]
        came = [swap(codes, "labels", mask) for mask in reversed(partners)]
        if step is not steps[-1]:
            codes = pl.pallas_call(
                functools.partial(merge_kernel, rows=rows, width=width),
                out_shape=coded_shape(rows, width),
                in_specs=[vmem] * (1 + len(came)),
                out_specs=vmem,
                compiler_params=params,
                name="merge",
            )(codes, *came)
    parts = pl.pallas_call(
        functools.partial(last_merge_kernel, rows=rows, width=width),
        out_shape=jax.ShapeDtypeStruct((rows, width), jnp.float32),
        in_specs=[vmem] * (1 + len(came)),
        out_specs=hbm,
        scratch_shapes=[
            pltpu.VMEM((rows, width), jnp.float32),
            pltpu.SemaphoreType.DMA((rows // TILE_ROWS,)),
        ],
        compiler_params=params,
        name="last_merge",
    )(codes, *came)
    return weights, momentum, parts.reshape(batches, group, width)


def solution(mesh):
    in_specs = (
        P("rows", None),
        P("rows", None),
        P("rows"),
        P(None, "rows"),
        P(("rows", "labels"), None),
        P(("rows", "labels"), None),
    )
    out_specs = (P(("rows", "labels"), None), P(("rows", "labels"), None), P(None, "rows", None))
    return jax.shard_map(
        per_device, mesh=mesh, in_specs=in_specs, out_specs=out_specs, check_vma=False
    )
```

```python
import functools
import math

import jax
import jax.numpy as jnp
from jax import lax
from jax.experimental import pallas as pl
from jax.experimental.pallas import tpu as pltpu
from jax.sharding import PartitionSpec as P

learn_rate = 0.001
decay_rate = 0.9
LANES = 128
NO_LABEL = 255
VMEM_LIMIT = 16 << 20
COLUMNS = 256
PARTS = 4
TILE_ROWS = 16
CODE_TOP = 32000.0
SMALLEST = 1e-30


def fetch(sources, targets, sems):
    copies = [pltpu.make_async_copy(s, t, sems.at[i]) for i, (s, t) in enumerate(zip(sources, targets))]
    for copy in copies:
        copy.start()
    return copies


def select_kernel(
    rows_hbm,
    features_hbm,
    labels_hbm,
    counts_hbm,
    out_ref,
    rows_ref,
    features_ref,
    labels_ref,
    counts_ref,
    sems,
    *,
    digits,
):
    slots, stored = labels_ref.shape
    batches, group = rows_ref.shape
    width = features_ref.shape[1]
    part = stored // PARTS
    bands = [pl.ds(i * part, part) for i in range(PARTS)]
    copies = fetch(
        (*[features_hbm.at[band] for band in bands], rows_hbm, labels_hbm, counts_hbm),
        (*[features_ref.at[band] for band in bands], rows_ref, labels_ref, counts_ref),
        sems,
    )
    copies[PARTS].wait()
    rows = batches * group
    one_hot = jnp.concatenate(
        [
            jnp.transpose(
                jnp.where(
                    lax.broadcasted_iota(jnp.int32, (stored, group), 0) == rows_ref[t : t + 1, :], 1.0, 0.0
                )
            )
            for t in range(batches)
        ],
        axis=0,
    ).astype(jnp.bfloat16)
    for copy in copies[:PARTS] + copies[PARTS + 1 :]:
        copy.wait()
    ids = labels_ref[...]
    used = lax.broadcasted_iota(jnp.int32, (slots, stored), 0) < counts_ref[...]
    table = [(ids >> (8 * i)) & 255 for i in range(digits - 1)]
    table.append(jnp.where(used, ids >> (8 * (digits - 1)), NO_LABEL))
    table = jnp.concatenate(table, axis=0).astype(jnp.float32).astype(jnp.bfloat16)
    codes = across(table, one_hot)
    codes = [codes[i * slots : (i + 1) * slots, :] for i in range(digits)]
    codes += [jnp.zeros((slots, rows), jnp.float32)] * (digits % 2)
    start = rows * (width // LANES)
    for i in range(0, digits, 2):
        out_ref[start : start + slots, :] = jnp.concatenate(codes[i : i + 2], axis=1).astype(jnp.bfloat16)
        start += slots
    chosen = jnp.dot(one_hot, features_ref[...], preferred_element_type=jnp.float32).astype(jnp.bfloat16)
    for j in range(width // LANES):
        out_ref[j * rows : (j + 1) * rows, :] = chosen[:, j * LANES : (j + 1) * LANES]


def prepare_kernel(weights_hbm, momentum_hbm, after_ref, weights_ref, decayed_ref, low_ref, sems):
    copies = fetch((weights_hbm, momentum_hbm), (weights_ref, decayed_ref), sems)
    copies[0].wait()
    low_ref[...] = weights_ref[...].astype(jnp.bfloat16)
    copies[1].wait()
    decayed_ref[...] = decay_rate * decayed_ref[...]


def ahead_kernel(weights_ref, decayed_ref, after_ref, ahead_ref):
    ahead_ref[...] = weights_ref[...] - learn_rate * decayed_ref[...]


def features_of(piece_refs, batch, batches, group, width):
    rows = batches * group
    starts = [j * rows + batch * group for j in range(width // LANES)]
    return jnp.concatenate(
        [jnp.concatenate([r[i : i + group, :] for r in piece_refs], axis=0) for i in starts], axis=1
    )


def ids_of(piece_refs, batches, group, width, slots, digits):
    rows = batches * group
    start = rows * (width // LANES)
    ids = []
    for r in piece_refs:
        total = 0.0
        for i in range(digits):
            at = start + slots * (i // 2)
            total = total + 256.0**i * r[at : at + slots, :].astype(jnp.float32)[:, rows * (i % 2) : rows * (i % 2 + 1)]
        ids.append(total)
    return [jnp.concatenate([t[:, b * group : (b + 1) * group] for t in ids], axis=1) for b in range(batches)]


def targets_of(ids, labels, base):
    slots, rows = ids.shape
    local = jnp.clip(ids - base, -1.0, float(labels)).astype(jnp.int32).astype(jnp.int16)
    label = lax.broadcasted_iota(jnp.int32, (labels, rows), 0).astype(jnp.int16)
    one, targets = jnp.ones((labels, rows), jnp.bfloat16), jnp.zeros((labels, rows), jnp.bfloat16)
    for k in range(slots):
        same = label == jnp.broadcast_to(local[k : k + 1, :], (labels, rows))
        targets = jnp.where(same, one, targets)
    return targets


def across(a, b):
    return lax.dot_general(a, b, (((1,), (1,)), ((), ())), preferred_element_type=jnp.float32)


def errors_of(logits, targets):
    return (1.0 / (1.0 + jnp.exp(-logits)) - targets.astype(jnp.float32)).astype(jnp.bfloat16)


def grads_of(errors, features):
    return jnp.dot(errors, features, preferred_element_type=jnp.float32)


def parts_kernel(base_ref, *refs, pieces, batches, group, slots, digits):
    piece_refs = refs[:pieces]
    ahead_ref, low_ref = refs[pieces : pieces + 2]
    *part_refs, first_ref, second_ref, targets_ref = refs[pieces + 2 :]
    share = pieces // len(part_refs)
    labels, width = low_ref.shape
    half = labels // 2
    base = base_ref[0].astype(jnp.float32)
    chunks = [slice(c, min(c + COLUMNS, width)) for c in range(0, width, COLUMNS)]

    def put(t, errors, low_weights):
        for c, low in zip(chunks, low_weights):
            summed = lax.dot_general(
                errors, low, (((0,), (0,)), ((), ())), preferred_element_type=jnp.float32
            )
            for p in range(pieces):
                start = (2 * (p % share) + t) * group
                part_refs[p // share][start : start + group, c] = summed[p * group : (p + 1) * group, :]

    ids = ids_of(piece_refs, batches, group, width, slots, digits)
    features = features_of(piece_refs, 0, batches, group, width)
    logits = [across(low_ref[i * half : (i + 1) * half, :], features) for i in range(2)]
    targets = targets_of(ids[0], labels, base)
    errors = errors_of(jnp.concatenate(logits, axis=0), targets)
    first_ref[...] = errors
    next_features = features_of(piece_refs, 1, batches, group, width)
    targets_ref[...] = targets_of(ids[1], labels, base)
    next_low = []
    for c in chunks:
        low = (ahead_ref[:, c] - learn_rate * grads_of(errors, features[:, c])).astype(jnp.bfloat16)
        next_low.append(low)
    whole = jnp.concatenate(next_low, axis=1)
    logits = jnp.concatenate([across(whole[i * half : (i + 1) * half, :], next_features) for i in range(2)], axis=0)
    put(0, errors, [low_ref[:, c] for c in chunks])
    errors = errors_of(logits, targets_ref[...])
    second_ref[...] = errors
    put(1, errors, next_low)


def update_kernel(errors_ref, *refs, batch, batches, group):
    piece_refs = refs[:-4]
    weights_ref, momentum_ref, weights_out, momentum_out = refs[-4:]
    features = features_of(piece_refs, batch, batches, group, weights_ref.shape[1])
    momentum = momentum_ref[...] if batch == 0 else decay_rate * momentum_ref[...]
    momentum = momentum + grads_of(errors_ref[...], features)
    momentum_out[...] = momentum
    weights_out[...] = weights_ref[...] - learn_rate * momentum


def encode(blocks, out_ref):
    rows = TILE_ROWS * len(blocks)
    lane = lax.broadcasted_iota(jnp.int32, (TILE_ROWS, LANES), 1)
    tile = jnp.zeros((TILE_ROWS, LANES), jnp.float32)
    for g, values in enumerate(blocks):
        top = jnp.maximum(jnp.max(jnp.abs(values), axis=1, keepdims=True), SMALLEST)
        power = jnp.ceil(jnp.log(top * (1.0 / CODE_TOP)) * (1.0 / math.log(2.0)))
        codes = jnp.round(values * jnp.exp2(-power)).astype(jnp.int32).astype(jnp.int16)
        for j in range(values.shape[1] // LANES):
            start = j * rows + g * TILE_ROWS
            out_ref[start : start + TILE_ROWS, :] = codes[:, j * LANES : (j + 1) * LANES]
        tile = jnp.where(lane == g, power, tile)
    out_ref[out_ref.shape[0] - TILE_ROWS :, :] = tile.astype(jnp.int32).astype(jnp.int16)


def decode(codes_ref, g, rows, width):
    scale = jnp.exp2(codes_ref[codes_ref.shape[0] - TILE_ROWS :, :].astype(jnp.float32)[:, g : g + 1])
    start = g * TILE_ROWS
    return jnp.concatenate(
        [
            codes_ref[j * rows + start : j * rows + start + TILE_ROWS, :].astype(jnp.float32) * scale
            for j in range(width // LANES)
        ],
        axis=1,
    )


def coded_shape(rows, width):
    return jax.ShapeDtypeStruct((rows * (width // LANES) + TILE_ROWS, LANES), jnp.int16)


def fold_kernel(kept_ref, received_ref, *out_refs, coded):
    rows, width = kept_ref.shape
    blocks = []
    for g in range(rows // TILE_ROWS):
        at = slice(g * TILE_ROWS, (g + 1) * TILE_ROWS)
        total = kept_ref[at, :] + (decode(received_ref, g, rows, width) if coded else received_ref[at, :])
        if len(out_refs) == 2 and at.stop <= rows // 2:
            out_refs[0][at, :] = total
        else:
            blocks.append(total)
    encode(blocks, out_refs[-1])


def merged(refs, g, rows, width):
    own, *came = [decode(r, g, rows, width) for r in refs]
    total = own + came[-1]
    if len(came) == 3:
        total = total + (came[1] + came[0])
    return total


def merge_kernel(*refs, rows, width):
    encode([merged(refs[:-1], g, rows, width) for g in range(rows // TILE_ROWS)], refs[-1])


def last_merge_kernel(*refs, rows, width):
    *came, out_hbm, out_ref, sems = refs
    copies = []
    for g in range(rows // TILE_ROWS):
        at = pl.ds(g * TILE_ROWS, TILE_ROWS)
        out_ref[at, :] = merged(came, g, rows, width)
        copies.append(pltpu.make_async_copy(out_ref.at[at], out_hbm.at[at], sems.at[g]))
        copies[-1].start()
    for copy in copies:
        copy.wait()


def swap(x, axis, mask):
    size = lax.axis_size(axis)
    return lax.ppermute(x, axis, [(i, i ^ mask) for i in range(size)])


def masks_of(axis):
    size = lax.axis_size(axis)
    return [1 << b for b in range(size.bit_length() - 1)]


def per_device(pool_features, pool_labels, pool_counts, batch_rows, weights, momentum):
    labels, width = weights.shape
    stored, slots = pool_labels.shape
    batches, group = batch_rows.shape
    pieces = lax.axis_size("rows")
    batch_size = pieces * group
    digits = 2 if pieces * lax.axis_size("labels") * labels <= NO_LABEL * 256 else 3
    device_index = lax.axis_index("rows") * lax.axis_size("labels") + lax.axis_index("labels")
    base = (device_index * labels).astype(jnp.int32).reshape(1)
    vmem = pl.BlockSpec(memory_space=pltpu.VMEM)
    hbm = pl.BlockSpec(memory_space=pltpu.HBM)
    params = pltpu.CompilerParams(vmem_limit_bytes=VMEM_LIMIT)

    own = pl.pallas_call(
        functools.partial(select_kernel, digits=digits),
        out_shape=jax.ShapeDtypeStruct(
            (batches * group * (width // LANES) + slots * ((digits + 1) // 2), LANES), jnp.bfloat16
        ),
        in_specs=[hbm] * 4,
        out_specs=vmem,
        scratch_shapes=[
            pltpu.VMEM(batch_rows.shape, jnp.int32),
            pltpu.VMEM(pool_features.shape, jnp.bfloat16),
            pltpu.VMEM((slots, stored), jnp.int32),
            pltpu.VMEM((1, stored), jnp.int32),
            pltpu.SemaphoreType.DMA((3 + PARTS,)),
        ],
        compiler_params=params,
        name="select_rows",
    )(*[pltpu.with_memory_space_constraint(a, pltpu.HBM) for a in (batch_rows, pool_features, pool_labels.T, pool_counts.reshape(1, stored))])

    weights, momentum, low_weights = pl.pallas_call(
        prepare_kernel,
        out_shape=(
            jax.ShapeDtypeStruct(weights.shape, jnp.float32),
            jax.ShapeDtypeStruct(momentum.shape, jnp.float32),
            jax.ShapeDtypeStruct(weights.shape, jnp.bfloat16),
        ),
        in_specs=[hbm, hbm, vmem],
        out_specs=(vmem,) * 3,
        scratch_shapes=[pltpu.SemaphoreType.DMA((2,))],
        compiler_params=params,
        cost_estimate=pl.CostEstimate(
            flops=0, transcendentals=0, bytes_accessed=18 * labels * width
        ),
        name="prepare",
    )(*[pltpu.with_memory_space_constraint(a, pltpu.HBM) for a in (weights, momentum)], own)

    gathered = [own]
    for mask in reversed(masks_of("rows")):
        came = [swap(g, "rows", mask) for g in gathered]
        if mask > 1:
            *came, low_weights = lax.optimization_barrier((*came, low_weights))
        gathered = gathered + came

    ahead = pl.pallas_call(
        ahead_kernel,
        out_shape=jax.ShapeDtypeStruct(weights.shape, jnp.float32),
        in_specs=[vmem] * 3,
        out_specs=vmem,
        compiler_params=params,
        cost_estimate=pl.CostEstimate(
            flops=2 * labels * width, transcendentals=0, bytes_accessed=12 * labels * width
        ),
        name="ahead",
    )(weights, momentum, gathered[pieces // 2 - 1])

    quarter = batches * batch_size // 4
    kept, moved, kept_theirs, moved_theirs, first, second = pl.pallas_call(
        functools.partial(
            parts_kernel, pieces=pieces, batches=batches, group=group, slots=slots, digits=digits
        ),
        out_shape=(
            *[jax.ShapeDtypeStruct((quarter, width), jnp.float32)] * 4,
            jax.ShapeDtypeStruct((labels, batch_size), jnp.bfloat16),
            jax.ShapeDtypeStruct((labels, batch_size), jnp.bfloat16),
        ),
        in_specs=[pl.BlockSpec(memory_space=pltpu.SMEM)] + [vmem] * (pieces + 2),
        out_specs=(vmem,) * 6,
        scratch_shapes=[pltpu.VMEM((labels, batch_size), jnp.bfloat16)],
        compiler_params=params,
        name="parts",
    )(base, *gathered, ahead, low_weights)

    def update(weights, momentum):
        for batch, errors in enumerate((first, second)):
            weights, momentum = pl.pallas_call(
                functools.partial(update_kernel, batch=batch, batches=batches, group=group),
                out_shape=(
                    jax.ShapeDtypeStruct(weights.shape, jnp.float32),
                    jax.ShapeDtypeStruct(momentum.shape, jnp.float32),
                ),
                in_specs=[vmem] * (pieces + 3),
                out_specs=(vmem,) * 2,
                compiler_params=params,
                cost_estimate=pl.CostEstimate(
                    flops=2 * batch_size * labels * width, transcendentals=0, bytes_accessed=16 * labels * width
                ),
                name=f"update_{batch}",
            )(errors, *gathered, weights, momentum)
        return weights, momentum

    def add(a, b, halve):
        rows = a.shape[0] // 2 if halve else a.shape[0]
        out = coded_shape(rows, width)
        return pl.pallas_call(
            functools.partial(fold_kernel, coded=b.dtype == jnp.int16),
            out_shape=(jax.ShapeDtypeStruct((rows, width), jnp.float32), out) if halve else out,
            in_specs=[vmem] * 2,
            out_specs=(vmem,) * 2 if halve else vmem,
            compiler_params=params,
            name="fold",
        )(a, b)

    masks = masks_of("rows")[1:]
    codes = add(moved, swap(moved_theirs, "rows", 1), False)
    received = swap(codes, "rows", masks[0])
    kept = kept + swap(kept_theirs, "rows", 1)
    received, kept, weights, momentum = lax.optimization_barrier((received, kept, *update(weights, momentum)))
    for mask in masks[1:]:
        kept, codes = add(kept, received, True)
        received = swap(codes, "rows", mask)
    rows = kept.shape[0]
    codes = add(kept, received, False)
    masks = masks_of("labels")
    steps = [masks[i : i + 2] for i in range(0, len(masks), 2)]
    for step in steps:
        partners = [step[0]] if len(step) == 1 else [step[0], step[1], step[0] | step[1]]
        came = [swap(codes, "labels", mask) for mask in reversed(partners)]
        if step is not steps[-1]:
            codes = pl.pallas_call(
                functools.partial(merge_kernel, rows=rows, width=width),
                out_shape=coded_shape(rows, width),
                in_specs=[vmem] * (1 + len(came)),
                out_specs=vmem,
                compiler_params=params,
                name="merge",
            )(codes, *came)
    parts = pl.pallas_call(
        functools.partial(last_merge_kernel, rows=rows, width=width),
        out_shape=jax.ShapeDtypeStruct((rows, width), jnp.float32),
        in_specs=[vmem] * (1 + len(came)),
        out_specs=hbm,
        scratch_shapes=[
            pltpu.VMEM((rows, width), jnp.float32),
            pltpu.SemaphoreType.DMA((rows // TILE_ROWS,)),
        ],
        compiler_params=params,
        name="last_merge",
    )(codes, *came)
    return weights, momentum, parts.reshape(batches, group, width)


def solution(mesh):
    in_specs = (
        P("rows", None),
        P("rows", None),
        P("rows"),
        P(None, "rows"),
        P(("rows", "labels"), None),
        P(("rows", "labels"), None),
    )
    out_specs = (P(("rows", "labels"), None), P(("rows", "labels"), None), P(None, "rows", None))
    return jax.shard_map(
        per_device, mesh=mesh, in_specs=in_specs, out_specs=out_specs, check_vma=False
    )
```
